32 devices in a mesh: member: 4 (over y, x), grid: 8 (over z, core).
Axes of the slice: x: 2, y: 2, z: 4, core: 2. Of those that a mesh axis runs over, the one named last changes fastest.
Arguments:
- latent: bfloat16 [4, 16384, 1024], P('member', 'grid'), may hold values from -6 to 6
- w_in: bfloat16 [1024, 1024], P(('member', 'grid')), may hold values from -0.1875 to 0.1875
- b_in: float32 [1024], replicated, may hold values from -3 to 3
- w_out: bfloat16 [100, 1024], replicated, may hold values from -0.1875 to 0.1875
- b_out: float32 [100], replicated, may hold values from -3 to 3
- targets: float32 [100, 16384], P(None, 'grid'), may hold values from -6 to 6
- var_weight: float32 [100], replicated, may hold values from 0.5 to 5
- plan: int32 [3, 4], replicated, may hold values from 0 to 3, as said below
Outputs:
- loss: float32 [], replicated
- grad_latent: bfloat16 [4, 16384, 1024], P('member', 'grid')
- grad_w_in: float32 [1024, 1024], P(('member', 'grid'))
- grad_b_in: float32 [1024], replicated
- grad_w_out: float32 [100, 1024], replicated
- grad_b_out: float32 [100], replicated
The draws below stay inside these ranges and needn't reach their ends.
Inputs may be any that keep to these rules, and one draw needn't show every extreme that they name: `plan`: each row is a perfect pairing of the 4 members: no member is its own partner, the partner of a member's partner is the member, and no pair occurs in two rows.
All inputs are finite; a program needn't handle non-finite values.
Results may differ from the reference program's by a relative error of at most 0.0095.
Values may be sent and summed in bfloat16 or wider, within the bound.
A program may use at most 128 MiB of HBM per device.

```python
import math
import jax
import jax.numpy as jnp
from jax import lax

L = 1024
V = 100
ROUNDS = 3
MEMBERS = 4
POINTS = 16384


def draw_plan(key, part):
    first_key, second_key = jax.random.split(jax.random.fold_in(key, 7))
    relabel = jax.random.permutation(first_key, MEMBERS).astype(jnp.int32)
    chosen = jax.random.permutation(second_key, MEMBERS - 1)[:ROUNDS].astype(jnp.int32)
    labels = jnp.arange(MEMBERS, dtype=jnp.int32)[None, :]
    rounds = chosen[:, None]
    partner = (2 * rounds - labels) % (MEMBERS - 1)
    partner = jnp.where(labels == rounds, MEMBERS - 1, partner)
    partner = jnp.where(labels == MEMBERS - 1, rounds, partner)
    mapped = relabel[partner]
    table = jnp.zeros((ROUNDS, MEMBERS), jnp.int32).at[:, relabel].set(mapped)
    return table.astype(jnp.int32)


def levels(stream_key, extent, cuts, least, largest):
    factor_of = 1.0
    for dim, parts in cuts:
        steps = jax.random.uniform(jax.random.fold_in(jax.random.fold_in(stream_key, 6), dim), (parts,), jnp.float32, least / len(cuts), largest / len(cuts))
        factor_of = factor_of * jnp.repeat(jnp.exp(steps), extent[dim] // parts).reshape((-1,) + (1,) * (len(extent) - 1 - dim))
    return factor_of


def normal_values(own_key, extent, width, most, pieces=(), kind=jnp.bfloat16):
    level = levels(own_key, extent, pieces, -0.22, 0.18) if pieces else 1.0
    entries = jax.random.normal(own_key, extent, jnp.float32) * width * level
    return jnp.minimum(jnp.maximum(entries, -most), most).astype(kind)


def setup_inputs(seed: int = 0) -> dict:
    key_list = jax.random.split(jax.random.key(seed), 9)
    return {
        "latent": normal_values(key_list[0], (MEMBERS, POINTS, L), 1.0, 6.0, ((0, 4), (1, 8))),
        "w_in": normal_values(key_list[1], (L, L), L ** -0.5, 0.1875, ((0, 32),)),
        "b_in": normal_values(key_list[2], (L,), 0.5, 3.0, (), jnp.float32),
        "w_out": normal_values(key_list[3], (V, L), L ** -0.5, 0.1875),
        "b_out": normal_values(key_list[4], (V,), 0.5, 3.0, (), jnp.float32),
        "targets": normal_values(key_list[5], (V, POINTS), 1.0, 6.0, ((1, 8),), jnp.float32),
        "var_weight": jnp.clip(jnp.exp(jax.random.uniform(key_list[6], (V,), jnp.float32, math.log(0.5), math.log(5.0))), 0.5, 5.0),
        "plan": draw_plan(jax.random.fold_in(key_list[8], 71), 0),
    }


DELTA = 0.25

def reference(latent, w_in, b_in, w_out, b_out, targets, var_weight, plan):
    place = jnp.arange(POINTS).astype(jnp.float32)
    area = jnp.cos(1.4 * (place + 0.5) / POINTS)
    scale_map = area[None, :] * var_weight[:, None]

    def forward(hidden_in):
        pre = jnp.dot(hidden_in, w_in, preferred_element_type=jnp.float32) + b_in[None, :]
        act = jax.nn.gelu(pre).astype(jnp.bfloat16)
        field = jnp.dot(w_out, act.T, preferred_element_type=jnp.float32) + b_out[:, None]
        return field
    fields = lax.map(forward, latent)

    def member_step(carry, member):
        acc_w1, acc_w2, acc_b1, acc_b2, acc_loss = carry
        hidden_in = latent[member]
        field = fields[member]
        others = fields[plan[:, member]]
        diff = field[None] - others
        root = jnp.sqrt(diff * diff + DELTA * DELTA)
        pairs = lax.optimization_barrier(jnp.sum(diff / root, axis=0))
        spread = lax.optimization_barrier(jnp.sum(root - DELTA, axis=0))
        miss = field - targets
        miss_root = jnp.sqrt(miss * miss + DELTA * DELTA)
        cot = scale_map * (miss / miss_root - pairs / ROUNDS)
        terms = scale_map * (miss_root - DELTA - spread / (2.0 * ROUNDS))
        cot_b = cot.astype(jnp.bfloat16)
        pre = jnp.dot(hidden_in, w_in, preferred_element_type=jnp.float32) + b_in[None, :]
        act = jax.nn.gelu(pre).astype(jnp.bfloat16)
        dact = jnp.dot(cot_b.T, w_out, preferred_element_type=jnp.float32)
        _, pull = jax.vjp(jax.nn.gelu, pre)
        dpre = pull(dact)[0]
        dpre_b = dpre.astype(jnp.bfloat16)
        grad_hidden = jnp.dot(dpre_b, w_in.T, preferred_element_type=jnp.float32).astype(jnp.bfloat16)
        acc_w1 = acc_w1 + jnp.dot(hidden_in.T, dpre_b, preferred_element_type=jnp.float32)
        acc_w2 = acc_w2 + jnp.dot(cot_b, act, preferred_element_type=jnp.float32)
        acc_b1 = acc_b1 + lax.optimization_barrier(jnp.sum(dpre, axis=0))
        acc_b2 = acc_b2 + lax.optimization_barrier(jnp.sum(cot, axis=1))
        acc_loss = acc_loss + jnp.sum(terms)
        return ((acc_w1, acc_w2, acc_b1, acc_b2, acc_loss), grad_hidden)
    start = (jnp.zeros((L, L), jnp.float32), jnp.zeros((V, L), jnp.float32), jnp.zeros((L,), jnp.float32), jnp.zeros((V,), jnp.float32), jnp.zeros((), jnp.float32))
    (acc_w1, acc_w2, acc_b1, acc_b2, acc_loss), grad_latent = lax.scan(member_step, start, jnp.arange(MEMBERS).astype(jnp.int32))
    kappa = 4.0 / jnp.sqrt(jnp.float32(MEMBERS * POINTS))
    loss = acc_loss / (MEMBERS * POINTS * V)
    return (loss, grad_latent, acc_w1 * kappa, acc_b1 * kappa, acc_w2 * kappa, acc_b2 * kappa)
```

```python
import functools
import math

import jax
import jax.numpy as jnp
from jax import lax
from jax.experimental import pallas as pl
from jax.experimental.pallas import tpu as pltpu
from jax.sharding import PartitionSpec as P

DELTA = 0.25


def make_fold(mine, partner_rows):

    def fold(carry, piece, start):
        count = piece.shape[0]
        labels = jnp.arange(count, dtype=jnp.int32)
        weights = jnp.sum((partner_rows[:, None] == labels[None, :]).astype(jnp.float32), axis=0)
        diff = mine[None] - piece
        root = jnp.sqrt(diff * diff + DELTA * DELTA)
        slope_sum = jnp.einsum("k,kvp->vp", weights, diff / root)
        spread_sum = jnp.einsum("k,kvp->vp", weights, root - DELTA)
        return (slope_sum, spread_sum)

    return fold


def shards(latent, w_in, b_in, w_out, b_out, targets, var_weight, plan):
    hidden_in = latent[0]
    points = hidden_in.shape[0]
    rounds = plan.shape[0]
    w_full = lax.all_gather(w_in, ("member", "grid"), axis=0, tiled=True)
    member = lax.axis_index("member")
    grid_index = lax.axis_index("grid")
    members = lax.axis_size("member")
    grid_count = lax.axis_size("grid")
    total = points * grid_count
    place = (grid_index * points + jnp.arange(points, dtype=jnp.int32)).astype(jnp.float32)
    area = jnp.cos(1.4 * (place + 0.5) / total)
    scale_map = area[None, :] * var_weight[:, None]
    partner_rows = lax.dynamic_index_in_dim(plan, member, 1, keepdims=False)
    pre = jnp.dot(hidden_in, w_full, preferred_element_type=jnp.float32) + b_in[None, :]
    act = jax.nn.gelu(pre).astype(jnp.bfloat16)
    field = jnp.dot(w_out, act.T, preferred_element_type=jnp.float32) + b_out[:, None]
    pre, act, field = (pre, act, field)
    fold_all = make_fold(field, partner_rows)
    slope_sum, spread_sum = fold_all(
        (
            jnp.zeros((w_out.shape[0], points), jnp.float32),
            jnp.zeros((w_out.shape[0], points), jnp.float32),
        ),
        lax.all_gather(field[None], "member", axis=0, tiled=True),
        jnp.int32(0),
    )
    miss = field - targets
    miss_root = jnp.sqrt(miss * miss + DELTA * DELTA)
    cot = scale_map * (miss / miss_root - slope_sum / rounds)
    terms = scale_map * (miss_root - DELTA - spread_sum / (2.0 * rounds))
    cot_b = cot.astype(jnp.bfloat16)
    dact = jnp.dot(cot_b.T, w_out, preferred_element_type=jnp.float32)
    _, pull = jax.vjp(jax.nn.gelu, pre)
    dpre = pull(dact)[0]
    dpre_b = dpre.astype(jnp.bfloat16)
    grad_hidden = jnp.dot(dpre_b, w_full.T, preferred_element_type=jnp.float32).astype(jnp.bfloat16)
    kappa = 4.0 / jnp.sqrt(jnp.float32(members * total))
    out_term = jnp.dot(cot_b, act, preferred_element_type=jnp.float32)
    sum_w2, sum_b2, sum_b1, sum_loss = lax.psum(
        (out_term, jnp.sum(cot, axis=1), jnp.sum(dpre, axis=0), jnp.sum(terms)), ("member", "grid")
    )
    row_count = w_in.shape[0]
    full_term = jnp.dot(hidden_in.T, dpre_b, preferred_element_type=jnp.float32)
    summed = lax.psum(full_term, ("member", "grid"))
    offset = (member * grid_count + grid_index) * row_count
    own_rows = lax.dynamic_slice_in_dim(summed, offset, row_count, 0)
    loss = sum_loss / (members * total * w_out.shape[0])
    return (
        loss,
        grad_hidden[None],
        own_rows * kappa,
        sum_b1 * kappa,
        sum_w2 * kappa,
        sum_b2 * kappa,
    )


TILE = 256
LANES = 128
BF = jnp.bfloat16
F32 = jnp.float32
I16 = jnp.int16
TOP = 32767.0
DIAG, ACROSS, DOWN, SELF = 0, 1, 2, 3


def dot(a, b, dims):
    return lax.dot_general(a, b, (dims, ((), ())), preferred_element_type=F32)


NN = ((1,), (0,))
NT = ((1,), (1,))
TN = ((0,), (0,))


def head_kernel(
    members, planes, lat_hbm, w_in, b_in, w_out, b_out, tgt_hbm, vw,
    gh, g_w1, g_b1, g_w2, g_b2, g_loss,
    lat, lat_t, w_buf, gp, act, dpre, wo, fown, fsend, frecv, csend, crecv, tgt, rowbuf, lane_sums,
    ot, op_send, op_recv, om, om_send, om_recv, oq, w2, sm, sp_recv, smm, smz,
    keep, part_sum, p_send, p_recv, d_send, d_recv, n_send, n_recv, z_send, z_recv,
    send_sem, recv_sem, local_sem,
):
    m = lax.axis_index("member")
    g = lax.axis_index("grid")
    z, c = g // 2, lax.rem(g, 2)
    other = 1 - c
    points = lat.shape[1]
    width = lat.shape[2]
    sub = points // members
    rows = w_in.shape[0]
    vars_ = w_out.shape[0]
    pad = wo.shape[0]
    latent = w_out.shape[1]
    total = points * planes * 2
    half = width // 2

    mem = (members - 1 - m, m + 1 - 2 * lax.rem(m, 2), m + 2 - 4 * (m // 2), m)
    zed = (z, z + 1 - 2 * lax.rem(z, 2), z + 2 - 4 * (z // 2), planes - 1 - z)

    partner = (m, z * 2 + other)

    def member_dev(s):
        return (mem[s], g)

    def z_dev(k):
        return (m, zed[k] * 2 + c)

    started = []

    def send(src, dst, dev):
        n = len(started)
        copy = pltpu.make_async_remote_copy(
            src_ref=src, dst_ref=dst, send_sem=send_sem.at[n], recv_sem=recv_sem.at[n],
            device_id=dev, device_id_type=pl.DeviceIdType.MESH,
        )
        copy.start()
        started.append(copy)
        return copy

    loads = []
    for s in (SELF, ACROSS, DOWN, DIAG):
        copy = pltpu.make_async_copy(
            lat_hbm.at[0, :, pl.ds(pl.multiple_of(mem[s] * width, LANES), width)], lat.at[s], local_sem.at[s]
        )
        copy.start()
        loads.append((s, copy))
    own = pltpu.make_async_copy(w_in, w_buf.at[m, z, c], local_sem.at[members])
    own.start()
    tgt_copy = pltpu.make_async_copy(
        tgt_hbm.at[:, pl.ds(pl.multiple_of(m * sub, LANES), sub)], tgt, local_sem.at[members + 1]
    )
    tgt_copy.start()

    barrier = pltpu.get_barrier_semaphore()
    peers = [partner] + [z_dev(k) for k in range(1, planes)] + [member_dev(s) for s in (DIAG, ACROSS, DOWN)]
    for dev in peers:
        pl.semaphore_signal(barrier, inc=1, device_id=dev, device_id_type=pl.DeviceIdType.MESH)
    pl.semaphore_wait(barrier, len(peers))

    near = {ACROSS: [], DOWN: []}
    far = []
    to_part = {s: [] for s in range(members)}
    z_copies = [None]

    def block(s, step):
        return w_buf.at[mem[s], zed[step], c]

    def hand_over(s, step):
        to_part[s].append(send(block(s, step), block(s, step), partner))

    def spread_block(step):
        if step > 0:
            z_copies[step].wait_recv()
        src = w_in if step == 0 else block(SELF, step)
        for s in (ACROSS, DOWN):
            near[s].append(send(src, block(SELF, step), member_dev(s)))
        to_part[SELF].append(send(src, block(SELF, step), partner))

    def relay_block(step):
        for s in (ACROSS, DOWN):
            near[s][step].wait_recv()
        s = ACROSS if step % 2 == 0 else DOWN
        far.append(send(block(s, step), block(s, step), member_dev(ACROSS + DOWN - s)))
        hand_over(ACROSS, step)
        hand_over(DOWN, step)

    def far_block(step):
        far[step].wait_recv()
        hand_over(DIAG, step)

    def transpose_next():
        s, copy = loads.pop(0)
        copy.wait()

        def body(t, carry):
            r0 = pl.multiple_of(t * 2 * TILE, 2 * TILE)
            turned = lat[s, pl.ds(r0, 2 * TILE), :].T
            lat_t[0, s, :, pl.ds(r0, 2 * TILE)] = turned[:half]
            lat_t[1, s, :, pl.ds(r0, 2 * TILE)] = turned[half:]
            return carry

        lax.fori_loop(0, points // (2 * TILE), body, 0)

    def contract(slots, first):
        for s in slots:
            for copy in to_part[s]:
                copy.wait_recv()
        big = 4 * TILE

        def body(t, carry):
            r0 = pl.multiple_of(t * big, big)
            acc = b_in[...] if first else gp[pl.ds(r0, big), :]
            for s in slots:
                acc = acc + dot(lat[s, pl.ds(r0, big), :], w_buf[mem[s]].reshape(width, latent), NN)
            gp[pl.ds(r0, big), :] = acc
            return carry

        lax.fori_loop(0, points // big, body, 0)

    for k in range(1, planes):
        z_copies.append(send(w_in, w_buf.at[m, z, c], z_dev(k)))
    spread_block(0)

    wo[...] = jnp.zeros_like(wo)
    wo[:vars_, :] = w_out[...]
    rowbuf[...] = jnp.zeros_like(rowbuf)
    rowbuf[0:1, :vars_] = b_out[...]
    rowbuf[1:2, :vars_] = vw[...]
    b_col = jnp.broadcast_to(rowbuf[0:1, :], (LANES, LANES)).T[:vars_]
    v_col = jnp.broadcast_to(rowbuf[1:2, :], (LANES, LANES)).T[:vars_]
    lane_sums[...] = jnp.zeros_like(lane_sums)
    ot[...] = jnp.zeros_like(ot)
    sm[...] = jnp.zeros_like(sm)
    own.wait()

    transpose_next()
    relay_block(0)
    spread_block(1)
    transpose_next()
    spread_block(2)
    relay_block(1)
    transpose_next()
    spread_block(3)
    relay_block(2)
    far_block(0)
    transpose_next()
    contract((SELF,), True)
    relay_block(3)
    far_block(1)
    far_block(2)
    contract((ACROSS, DOWN), False)
    far_block(3)
    for copy in to_part[DIAG]:
        copy.wait_recv()

    c0 = math.sqrt(2.0 / math.pi)
    parts = sub // TILE
    f_copies = {}
    eps = DELTA * DELTA
    c_copies = {}
    sums = {"b": jnp.zeros((vars_, LANES), F32), "l": jnp.zeros((vars_, LANES), F32)}

    def forward_tile(part, s):
        r0 = pl.multiple_of(mem[s] * sub + part * TILE, TILE)
        x = dot(lat[DIAG, pl.ds(r0, TILE), :], w_buf[mem[DIAG]].reshape(width, latent), NN)
        x = x + gp[pl.ds(r0, TILE), :]
        sq = x * x
        cdf = 0.5 + 0.5 * jnp.tanh(x * (c0 + (0.044715 * c0) * sq))
        out = x * cdf
        act[pl.ds(r0, TILE), :] = out.astype(BF)
        gp[pl.ds(r0, TILE), :] = cdf + (out * (1.0 - cdf)) * (2.0 * c0 + (6.0 * 0.044715 * c0) * sq)
        field = dot(wo[...], act[pl.ds(r0, TILE), :], NT)
        if s == SELF:
            fown[part] = field[:vars_]
        else:
            peak = jnp.max(jnp.abs(field), axis=0, keepdims=True)
            code = jnp.floor(jnp.sqrt(peak) * 64.0) + 2.0
            scale = (code * code) * (1.0 / 4096.0)
            coded = jnp.round(field * (TOP / scale))
            at = lax.broadcasted_iota(jnp.int32, (pad, TILE), 0)
            coded = jnp.where(at == vars_, jnp.broadcast_to(code, (pad, TILE)), coded)
            fsend[part, s] = coded.astype(jnp.int32).astype(I16)
            f_copies[part, s] = send(fsend.at[part, s], frecv.at[part, s], member_dev(s))

    def score(part):
        for s in (DIAG, ACROSS, DOWN):
            f_copies[part, s].wait_recv()
        b_sum, l_sum = sums["b"], sums["l"]
        for at in range(TILE // LANES):
            cols = slice(at * LANES, (at + 1) * LANES)
            first = part * TILE + at * LANES
            place = lax.broadcasted_iota(jnp.int32, (1, LANES), 1) + (g * points + m * sub + first)
            area = jnp.cos(1.4 * (place.astype(F32) + 0.5) / total)
            scale = v_col * area
            f = []
            for s in (DIAG, ACROSS, DOWN):
                coded = frecv[part, s, :, cols].astype(jnp.int32).astype(F32)
                code = coded[vars_:vars_ + 1]
                f.append(coded[:vars_] * ((code * code) * (1.0 / (4096.0 * TOP))))
            f.append(fown[part, :, cols])
            goal = tgt[:, first:first + LANES] - b_col
            pairs = [None] * members
            spread = jnp.zeros((vars_, LANES), F32)
            for i in range(members):
                for j in range(i + 1, members):
                    d = f[i] - f[j]
                    q = d * d + eps
                    inv = lax.rsqrt(q)
                    slope = d * inv
                    spread += q * inv - DELTA
                    pairs[i] = slope if pairs[i] is None else pairs[i] + slope
                    pairs[j] = -slope if pairs[j] is None else pairs[j] - slope
            miss_sum = jnp.zeros((vars_, LANES), F32)
            for s in range(members):
                d = f[s] - goal
                q = d * d + eps
                inv = lax.rsqrt(q)
                miss_sum += q * inv - DELTA
                cot = scale * (d * inv - pairs[s] * (1.0 / (members - 1)))
                b_sum += cot
                if s == SELF:
                    crecv[part, SELF, :, cols] = cot.astype(BF)
                else:
                    csend[part, s, :, cols] = cot.astype(BF)
            l_sum += scale * (miss_sum - spread * (1.0 / (members - 1)))
        sums["b"], sums["l"] = b_sum, l_sum
        for s in (DIAG, ACROSS, DOWN):
            c_copies[part, s] = send(csend.at[part, s], crecv.at[part, s], member_dev(s))

    tgt_copy.wait()
    for part in range(parts):
        for s in (DIAG, ACROSS, DOWN):
            forward_tile(part, s)
        if part > 0:
            score(part - 1)
        forward_tile(part, SELF)
    score(parts - 1)
    lane_sums[:vars_, :] = sums["b"]
    sm[1:2, :LANES] = jnp.sum(lane_sums[...].T, axis=0, keepdims=True)
    sm[1:2, LANES:2 * LANES] = jnp.sum(sums["l"], axis=0, keepdims=True)

    col = jnp.zeros((1, latent), F32)
    for part in range(parts):
        for s in (SELF, ACROSS, DOWN, DIAG):
            if s != SELF:
                c_copies[part, s].wait_recv()
            r0 = pl.multiple_of(mem[s] * sub + part * TILE, TILE)
            cot_b = crecv[part, s]
            d = dot(cot_b, w_out[...], TN) * gp[pl.ds(r0, TILE), :]
            dpre[pl.ds(r0, TILE), :] = d.astype(BF)
            ot[:vars_, :] += dot(cot_b, act[pl.ds(r0, TILE), :], NN)
            col += jnp.sum(d, axis=0, keepdims=True)
    sm[0:1, :] = col

    share = ot.shape[0] // (2 * planes)
    first_half = pl.multiple_of(other * (planes * share), share)
    op_send[...] = ot[pl.ds(first_half, planes * share), :].astype(BF)
    op_copy = send(op_send, op_recv, partner)
    sp_copy = send(sm, sp_recv, partner)

    p_copies = {}
    d_copies = {}
    n_copies = {}
    far_half = 1 - z // 2
    halves = (far_half, z // 2)
    pairs_of = ((DIAG, ACROSS), (DOWN, SELF))

    def chunk(h, pair):
        n = h * 2 + pair
        lo = pair * 2
        left = lat_t[halves[h], lo:lo + 2].reshape(width, points)
        keep[...] = dot(left, dpre[...], NN).reshape(2, 2, 2, rows, latent)
        p_send[n] = keep[:, :, other].astype(BF)
        part_sum[h, lo:lo + 2] = keep[:, :, c]
        p_copies[n] = send(p_send.at[n], p_recv.at[n], partner)

    def fold(h, pair):
        n = h * 2 + pair
        p_copies[n].wait_recv()
        lo = pair * 2
        both = part_sum[h, lo:lo + 2] + p_recv[n].astype(F32)
        if pair == 0:
            d_send[h] = both[0].astype(BF)
            d_copies[h] = [
                send(d_send.at[h, j], d_recv.at[h, j], member_dev(ACROSS + j)) for j in range(2)
            ]
            n_send[h, 0, 0] = both[1, 0].astype(BF)
            n_copies[h, ACROSS, 0] = send(n_send.at[h, 0, 0], n_recv.at[h, 0, 0], member_dev(ACROSS))
            part_sum[h, ACROSS, 1] = both[1, 1]
        else:
            n_send[h, 1, 1] = both[0, 1].astype(BF)
            n_copies[h, DOWN, 1] = send(n_send.at[h, 1, 1], n_recv.at[h, 1, 1], member_dev(DOWN))
            part_sum[h, DOWN, 0] = both[0, 0]
            part_sum[h, SELF] = both[1]

    def relay_sum(h):
        for s, j in ((DOWN, 0), (ACROSS, 1)):
            d_copies[h][j].wait_recv()
            n_send[h, s - 1, j] = (part_sum[h, s, j] + d_recv[h, j].astype(F32)).astype(BF)
            n_copies[h, s, j] = send(n_send.at[h, s - 1, j], n_recv.at[h, s - 1, j], member_dev(s))

    def plane_sum(h):
        for s in (ACROSS, DOWN):
            for j in range(2):
                n_copies[h, s, j].wait_recv()
        part_sum[h, SELF] = (part_sum[h, SELF] + n_recv[h, 0].astype(F32)) + n_recv[h, 1].astype(F32)

    side = lax.rem(z, 2)
    zz_copies = {}

    def to_plane(k):
        h = 0 if k > 1 else 1
        j = side if k == 2 else 1 - side
        z_send[k - 1] = part_sum[h, SELF, j].astype(BF)
        zz_copies[k] = send(z_send.at[k - 1], z_recv.at[k - 1], z_dev(k))

    def hidden_grad(ch):
        w = w_buf[ch].reshape(width, latent)
        gh[0, :, ch * width:(ch + 1) * width] = dot(dpre[...], w, NT).astype(BF)

    chunk(0, 0)
    chunk(0, 1)
    fold(0, 0)
    chunk(1, 0)
    fold(0, 1)
    op_copy.wait_recv()
    mine = pl.multiple_of(c * (planes * share), share)
    om[...] = (ot[pl.ds(mine, planes * share), :] + op_recv[...].astype(F32)).reshape(planes, share, latent)
    om_send[...] = om[...].astype(BF)
    om_copies = [send(om_send.at[zed[k]], om_recv.at[k - 1], z_dev(k)) for k in range(1, planes)]
    sp_copy.wait_recv()
    smm[m] = sm[...] + sp_recv[...]
    sm_copies = [send(smm.at[m], smm.at[m], member_dev(s)) for s in (DIAG, ACROSS, DOWN)]
    chunk(1, 1)
    relay_sum(0)
    fold(1, 0)
    fold(1, 1)
    hidden_grad(0)
    acc = om[z]
    for k in range(1, planes):
        om_copies[k - 1].wait_recv()
        acc += om_recv[k - 1].astype(F32)
    oq[m] = acc.astype(BF)
    oq_copies = [send(oq.at[m], oq.at[m], member_dev(s)) for s in (DIAG, ACROSS, DOWN)]
    for copy in sm_copies:
        copy.wait_recv()
    acc = smm[0]
    for k in range(1, members):
        acc += smm[k]
    smz[z] = acc
    sz_copies = [send(smz.at[z], smz.at[z], z_dev(k)) for k in range(1, planes)]
    plane_sum(0)
    to_plane(2)
    to_plane(3)
    hidden_grad(1)
    relay_sum(1)
    hidden_grad(2)
    for copy in oq_copies:
        copy.wait_recv()
    acc = oq[0].astype(F32)
    for k in range(1, members):
        acc += oq[k].astype(F32)
    w2[c, z] = acc.astype(BF)
    w2_copies = [send(w2.at[c, z], w2.at[c, z], z_dev(k)) for k in range(1, planes)]
    hidden_grad(3)
    plane_sum(1)
    to_plane(1)
    part_sum[1, SELF, 0] = part_sum[1, SELF, side]

    kappa = 4.0 / math.sqrt(members * total)
    for copy in sz_copies:
        copy.wait_recv()
    acc = smz[0]
    for k in range(1, planes):
        acc += smz[k]
    acc = acc * kappa
    g_b1[...] = acc[0:1, :]
    g_b2[...] = acc[1:2, :vars_]
    g_loss[...] = jnp.sum(acc[1:2, LANES:2 * LANES], axis=1, keepdims=True) * (1.0 / (kappa * members * total * vars_))
    for copy in w2_copies:
        copy.wait_recv()
    half_copy = send(w2.at[c], w2.at[c], partner)

    acc = part_sum[1, SELF, 0]
    for k in (2, 3, 1):
        zz_copies[k].wait_recv()
        acc += z_recv[k - 1].astype(F32)
    g_w1[...] = acc * kappa
    half_copy.wait_recv()
    g_w2[...] = w2[...].reshape(2 * planes * share, latent)[:vars_].astype(F32) * kappa
    for copy in started:
        copy.wait_send()


def store_kernel(*refs):
    count = len(refs) // 2
    copies = []
    for n in range(count):
        copy = pltpu.make_async_copy(refs[n], refs[count + n], refs[2 * count].at[n])
        copy.start()
        copies.append(copy)
    for copy in copies:
        copy.wait()


def fast(latent, w_in, b_in, w_out, b_out, targets, var_weight, plan):
    members = lax.axis_size("member")
    grid = lax.axis_size("grid")
    planes = grid // 2
    points, width = latent.shape[1], latent.shape[2]
    rows = w_in.shape[0]
    vars_ = w_out.shape[0]
    sub = points // members
    cw = width // members
    parts = sub // TILE
    share = 16 * pl.cdiv(vars_, 32 * planes)
    pad = 8 * pl.cdiv(vars_ + 1, 8)
    n_sems = (planes - 1) * 4 + planes * 10 + (members - 1) * (4 + 2 * parts) + 2 * members + 24
    vmem = pl.BlockSpec(memory_space=pltpu.VMEM)
    hbm = pl.BlockSpec(memory_space=pl.ANY)
    V = pltpu.VMEM
    block = (rows, width)
    scratch = [
        V((members, points, cw), BF), V((2, members, cw // 2, points), BF), V((members, planes, 2, *block), BF),
        V((points, width), F32), V((points, width), BF), V((points, width), BF),
        V((pad, width), BF), V((parts, vars_, TILE), F32),
        V((parts, members - 1, pad, TILE), I16), V((parts, members - 1, pad, TILE), I16),
        V((parts, members - 1, vars_, TILE), BF), V((parts, members, vars_, TILE), BF), V((vars_, sub), F32),
        V((8, LANES), F32), V((LANES, LANES), F32),
        V((2 * planes * share, width), F32), V((planes * share, width), BF), V((planes * share, width), BF),
        V((planes, share, width), F32), V((planes, share, width), BF), V((planes - 1, share, width), BF),
        V((members, share, width), BF), V((2, planes, share, width), BF),
        V((2, width), F32), V((2, width), F32), V((members, 2, width), F32), V((planes, 2, width), F32),
        V((2, 2, 2, *block), F32), V((2, members, 2, *block), F32),
        V((4, 2, 2, *block), BF), V((4, 2, 2, *block), BF),
        V((2, 2, *block), BF), V((2, 2, *block), BF), V((2, 2, 2, *block), BF), V((2, 2, 2, *block), BF),
        V((planes - 1, *block), BF), V((planes - 1, *block), BF),
        pltpu.SemaphoreType.DMA((n_sems,)), pltpu.SemaphoreType.DMA((n_sems,)),
        pltpu.SemaphoreType.DMA((members + 2,)),
    ]
    S = jax.ShapeDtypeStruct
    shapes = [
        ((1, points, width), BF), ((rows, width), F32), ((1, width), F32),
        ((vars_, width), F32), ((1, vars_), F32), ((1, 1), F32),
    ]
    held = pl.pallas_call(
        functools.partial(head_kernel, members, planes),
        out_shape=[pltpu.VMEM(*s) for s in shapes],
        in_specs=[hbm, vmem, vmem, vmem, vmem, hbm, vmem],
        out_specs=[vmem] * len(shapes),
        scratch_shapes=scratch,
        compiler_params=pltpu.CompilerParams(
            collective_id=0, has_side_effects=True, vmem_limit_bytes=55 * 1024 * 1024
        ),
    )(latent, w_in, b_in[None], w_out, b_out[None], targets, var_weight[None])
    gh, g_w1, g_b1, g_w2, g_b2, g_loss = pl.pallas_call(
        store_kernel,
        out_shape=[S(*s) for s in shapes],
        in_specs=[hbm] * len(shapes),
        out_specs=[hbm] * len(shapes),
        scratch_shapes=[pltpu.SemaphoreType.DMA((len(shapes),))],
        compiler_params=pltpu.CompilerParams(has_side_effects=True, vmem_limit_bytes=1024 * 1024),
    )(*[pltpu.with_memory_space_constraint(h, pltpu.VMEM) for h in held])
    return g_loss[0, 0], gh, g_w1, g_b1[0], g_w2, g_b2[0]


def local(latent, w_in, b_in, w_out, b_out, targets, var_weight, plan):
    members = lax.axis_size("member")
    grid = lax.axis_size("grid")
    points, width = latent.shape[1], latent.shape[2]
    whole_plan = plan.shape[0] == members - 1
    tiled = (
        w_in.shape[0] % 16 == 0 and grid == 8 and members == 4
        and points % (members * TILE) == 0 and width % (2 * members * LANES) == 0
        and width // members == grid * w_in.shape[0] and w_out.shape[0] < LANES
        and points * width <= 2048 * 1024
    )
    run = fast if whole_plan and tiled else shards
    return run(latent, w_in, b_in, w_out, b_out, targets, var_weight, plan)


def solution(mesh):
    placed = (
        P("member", "grid", None),
        P(("member", "grid"), None),
        P(),
        P(),
        P(),
        P(None, "grid"),
        P(),
        P(),
    )
    return jax.shard_map(
        local,
        mesh=mesh,
        in_specs=placed,
        out_specs=(P(), P("member", "grid", None), P(("member", "grid"), None), P(), P(), P()),
        check_vma=False,
    )
```

```python
import functools
import math

import jax
import jax.numpy as jnp
from jax import lax
from jax.experimental import pallas as pl
from jax.experimental.pallas import tpu as pltpu
from jax.sharding import PartitionSpec as P

DELTA = 0.25


def make_fold(mine, partner_rows):

    def fold(carry, piece, start):
        count = piece.shape[0]
        labels = jnp.arange(count, dtype=jnp.int32)
        weights = jnp.sum((partner_rows[:, None] == labels[None, :]).astype(jnp.float32), axis=0)
        diff = mine[None] - piece
        root = jnp.sqrt(diff * diff + DELTA * DELTA)
        slope_sum = jnp.einsum("k,kvp->vp", weights, diff / root)
        spread_sum = jnp.einsum("k,kvp->vp", weights, root - DELTA)
        return (slope_sum, spread_sum)

    return fold


def shards(latent, w_in, b_in, w_out, b_out, targets, var_weight, plan):
    hidden_in = latent[0]
    points = hidden_in.shape[0]
    rounds = plan.shape[0]
    w_full = lax.all_gather(w_in, ("member", "grid"), axis=0, tiled=True)
    member = lax.axis_index("member")
    grid_index = lax.axis_index("grid")
    members = lax.axis_size("member")
    grid_count = lax.axis_size("grid")
    total = points * grid_count
    place = (grid_index * points + jnp.arange(points, dtype=jnp.int32)).astype(jnp.float32)
    area = jnp.cos(1.4 * (place + 0.5) / total)
    scale_map = area[None, :] * var_weight[:, None]
    partner_rows = lax.dynamic_index_in_dim(plan, member, 1, keepdims=False)
    pre = jnp.dot(hidden_in, w_full, preferred_element_type=jnp.float32) + b_in[None, :]
    act = jax.nn.gelu(pre).astype(jnp.bfloat16)
    field = jnp.dot(w_out, act.T, preferred_element_type=jnp.float32) + b_out[:, None]
    pre, act, field = (pre, act, field)
    fold_all = make_fold(field, partner_rows)
    slope_sum, spread_sum = fold_all(
        (
            jnp.zeros((w_out.shape[0], points), jnp.float32),
            jnp.zeros((w_out.shape[0], points), jnp.float32),
        ),
        lax.all_gather(field[None], "member", axis=0, tiled=True),
        jnp.int32(0),
    )
    miss = field - targets
    miss_root = jnp.sqrt(miss * miss + DELTA * DELTA)
    cot = scale_map * (miss / miss_root - slope_sum / rounds)
    terms = scale_map * (miss_root - DELTA - spread_sum / (2.0 * rounds))
    cot_b = cot.astype(jnp.bfloat16)
    dact = jnp.dot(cot_b.T, w_out, preferred_element_type=jnp.float32)
    _, pull = jax.vjp(jax.nn.gelu, pre)
    dpre = pull(dact)[0]
    dpre_b = dpre.astype(jnp.bfloat16)
    grad_hidden = jnp.dot(dpre_b, w_full.T, preferred_element_type=jnp.float32).astype(jnp.bfloat16)
    kappa = 4.0 / jnp.sqrt(jnp.float32(members * total))
    out_term = jnp.dot(cot_b, act, preferred_element_type=jnp.float32)
    sum_w2, sum_b2, sum_b1, sum_loss = lax.psum(
        (out_term, jnp.sum(cot, axis=1), jnp.sum(dpre, axis=0), jnp.sum(terms)), ("member", "grid")
    )
    row_count = w_in.shape[0]
    full_term = jnp.dot(hidden_in.T, dpre_b, preferred_element_type=jnp.float32)
    summed = lax.psum(full_term, ("member", "grid"))
    offset = (member * grid_count + grid_index) * row_count
    own_rows = lax.dynamic_slice_in_dim(summed, offset, row_count, 0)
    loss = sum_loss / (members * total * w_out.shape[0])
    return (
        loss,
        grad_hidden[None],
        own_rows * kappa,
        sum_b1 * kappa,
        sum_w2 * kappa,
        sum_b2 * kappa,
    )


TILE = 256
LANES = 128
BF = jnp.bfloat16
F32 = jnp.float32
I16 = jnp.int16
TOP = 32767.0
DIAG, ACROSS, DOWN, SELF = 0, 1, 2, 3


def dot(a, b, dims):
    return lax.dot_general(a, b, (dims, ((), ())), preferred_element_type=F32)


NN = ((1,), (0,))
NT = ((1,), (1,))
TN = ((0,), (0,))


def head_kernel(
    members, planes, lat_hbm, w_in, b_in_hbm, w_out_hbm, b_out_hbm, tgt_hbm, vw_hbm,
    gh, g_w1, g_b1, g_w2, g_b2, g_loss,
    lat, lat_t, w_buf, gp, act, dpre, b_in, w_out, b_out, vw, wo, fown, fsend, frecv, csend, crecv, tgt, rowbuf, lane_sums,
    ot, op_send, op_recv, om, om_send, om_recv, oq, w2, sm, sp_recv, smm, smz,
    keep, part_sum, p_send, p_recv, d_send, d_recv, n_send, n_recv, z_send, z_recv,
    send_sem, recv_sem, local_sem,
):
    m = lax.axis_index("member")
    g = lax.axis_index("grid")
    z, c = g // 2, lax.rem(g, 2)
    other = 1 - c
    points = lat.shape[1]
    width = lat.shape[2]
    sub = points // members
    rows = w_in.shape[0]
    vars_ = w_out.shape[0]
    pad = wo.shape[0]
    latent = w_out.shape[1]
    total = points * planes * 2
    half = width // 2

    mem = (members - 1 - m, m + 1 - 2 * lax.rem(m, 2), m + 2 - 4 * (m // 2), m)
    zed = (z, z + 1 - 2 * lax.rem(z, 2), z + 2 - 4 * (z // 2), planes - 1 - z)

    partner = (m, z * 2 + other)

    def member_dev(s):
        return (mem[s], g)

    def z_dev(k):
        return (m, zed[k] * 2 + c)

    started = []

    def send(src, dst, dev):
        n = len(started)
        copy = pltpu.make_async_remote_copy(
            src_ref=src, dst_ref=dst, send_sem=send_sem.at[n], recv_sem=recv_sem.at[n],
            device_id=dev, device_id_type=pl.DeviceIdType.MESH,
        )
        copy.start()
        started.append(copy)
        return copy

    barrier = pltpu.get_barrier_semaphore()
    peers = [partner] + [z_dev(k) for k in range(1, planes)] + [member_dev(s) for s in (DIAG, ACROSS, DOWN)]
    for dev in peers:
        pl.semaphore_signal(barrier, inc=1, device_id=dev, device_id_type=pl.DeviceIdType.MESH)
    pl.semaphore_wait(barrier, len(peers))

    near = {ACROSS: [], DOWN: []}
    far = []
    to_part = {s: [] for s in range(members)}
    z_copies = [None]

    def block(s, step):
        return w_buf.at[mem[s], zed[step], c]

    def hand_over(s, step):
        to_part[s].append(send(block(s, step), block(s, step), partner))

    def spread_block(step):
        if step > 0:
            z_copies[step].wait_recv()
        if step == 2:
            z_copies.append(send(block(SELF, 2), block(SELF, 2), z_dev(1)))
        src = w_in if step == 0 else block(SELF, step)
        for s in (ACROSS, DOWN):
            near[s].append(send(src, block(SELF, step), member_dev(s)))
        to_part[SELF].append(send(src, block(SELF, step), partner))

    def relay_block(step):
        for s in (ACROSS, DOWN):
            near[s][step].wait_recv()
        s = ACROSS if step % 2 == 0 else DOWN
        far.append(send(block(s, step), block(s, step), member_dev(ACROSS + DOWN - s)))
        hand_over(ACROSS, step)
        hand_over(DOWN, step)

    def far_block(step):
        far[step].wait_recv()
        hand_over(DIAG, step)

    def transpose_next():
        s, copy = loads.pop(0)
        copy.wait()

        def body(t, carry):
            r0 = pl.multiple_of(t * 2 * TILE, 2 * TILE)
            turned = lat[s, pl.ds(r0, 2 * TILE), :].T
            lat_t[0, s, :, pl.ds(r0, 2 * TILE)] = turned[:half]
            lat_t[1, s, :, pl.ds(r0, 2 * TILE)] = turned[half:]
            return carry

        lax.fori_loop(0, points // (2 * TILE), body, 0)

    def contract(slots, first):
        for s in slots:
            for copy in to_part[s]:
                copy.wait_recv()
        big = 4 * TILE

        def body(t, carry):
            r0 = pl.multiple_of(t * big, big)
            acc = b_in[...] if first else gp[pl.ds(r0, big), :]
            for s in slots:
                acc = acc + dot(lat[s, pl.ds(r0, big), :], w_buf[mem[s]].reshape(width, latent), NN)
            gp[pl.ds(r0, big), :] = acc
            return carry

        lax.fori_loop(0, points // big, body, 0)

    z_copies.append(send(w_in, w_buf.at[m, z, c], z_dev(1)))
    z_copies.append(send(w_in, w_buf.at[m, z, c], z_dev(2)))
    spread_block(0)

    own = pltpu.make_async_copy(w_in, w_buf.at[m, z, c], local_sem.at[members])
    own.start()
    loads = []
    for s in (SELF, ACROSS, DOWN, DIAG):
        copy = pltpu.make_async_copy(
            lat_hbm.at[0, :, pl.ds(pl.multiple_of(mem[s] * width, LANES), width)], lat.at[s], local_sem.at[s]
        )
        copy.start()
        loads.append((s, copy))
    tgt_copy = pltpu.make_async_copy(
        tgt_hbm.at[:, pl.ds(pl.multiple_of(m * sub, LANES), sub)], tgt, local_sem.at[members + 1]
    )
    tgt_copy.start()
    small_copies = []
    for n, (src, dst) in enumerate(((b_out_hbm, b_out), (vw_hbm, vw), (w_out_hbm, w_out), (b_in_hbm, b_in))):
        copy = pltpu.make_async_copy(src, dst, local_sem.at[members + 2 + n])
        copy.start()
        small_copies.append(copy)


    wo[...] = jnp.zeros_like(wo)
    for copy in small_copies:
        copy.wait()
    wo[:vars_, :] = w_out[...]
    rowbuf[...] = jnp.zeros_like(rowbuf)
    rowbuf[0:1, :vars_] = b_out[...]
    rowbuf[1:2, :vars_] = vw[...]
    b_col = jnp.broadcast_to(rowbuf[0:1, :], (LANES, LANES)).T[:vars_]
    v_col = jnp.broadcast_to(rowbuf[1:2, :], (LANES, LANES)).T[:vars_]
    lane_sums[...] = jnp.zeros_like(lane_sums)
    ot[...] = jnp.zeros_like(ot)
    sm[...] = jnp.zeros_like(sm)
    csend[...] = jnp.zeros_like(csend)
    own.wait()

    transpose_next()
    relay_block(0)
    spread_block(1)
    transpose_next()
    spread_block(2)
    relay_block(1)
    transpose_next()
    spread_block(3)
    relay_block(2)
    far_block(0)
    transpose_next()
    contract((SELF,), True)
    relay_block(3)
    far_block(1)
    far_block(2)
    contract((ACROSS, DOWN), False)
    far_block(3)
    for copy in to_part[DIAG]:
        copy.wait_recv()

    c0 = math.sqrt(2.0 / math.pi)
    parts = sub // TILE
    f_copies = {}
    eps = DELTA * DELTA
    c_copies = {}
    sums = {"b": jnp.zeros((vars_, LANES), F32), "l": jnp.zeros((vars_, LANES), F32)}

    def activate(part, s):
        r0 = pl.multiple_of(mem[s] * sub + part * TILE, TILE)
        x = dot(lat[DIAG, pl.ds(r0, TILE), :], w_buf[mem[DIAG]].reshape(width, latent), NN)
        x = x + gp[pl.ds(r0, TILE), :]
        sq = x * x
        cdf = 0.5 + 0.5 * jnp.tanh(x * (c0 + (0.044715 * c0) * sq))
        out = x * cdf
        rounded = out.astype(BF)
        act[pl.ds(r0, TILE), :] = rounded
        gp[pl.ds(r0, TILE), :] = cdf + (out * (1.0 - cdf)) * (2.0 * c0 + (6.0 * 0.044715 * c0) * sq)
        return rounded

    def project(part, s, rounded):
        field = dot(wo[...], rounded, NT)
        if s == SELF:
            fown[part] = field[:vars_]
        else:
            peak = jnp.max(jnp.abs(field), axis=0, keepdims=True)
            code = jnp.floor(jnp.sqrt(peak) * 64.0) + 2.0
            scale = (code * code) * (1.0 / 4096.0)
            coded = jnp.round(field * (TOP / scale))
            at = lax.broadcasted_iota(jnp.int32, (pad, TILE), 0)
            coded = jnp.where(at == vars_, jnp.broadcast_to(code, (pad, TILE)), coded)
            fsend[part, s] = coded.astype(jnp.int32).astype(I16)

    def send_field(part, s):
        if s != SELF:
            f_copies[part, s] = send(fsend.at[part, s], frecv.at[part, s], member_dev(s))

    def score(part):
        for s in (DIAG, ACROSS, DOWN):
            f_copies[part, s].wait_recv()
        b_sum, l_sum = sums["b"], sums["l"]
        for at in range(TILE // LANES):
            cols = slice(at * LANES, (at + 1) * LANES)
            first = part * TILE + at * LANES
            place = lax.broadcasted_iota(jnp.int32, (1, LANES), 1) + (g * points + m * sub + first)
            area = jnp.cos(1.4 * (place.astype(F32) + 0.5) / total)
            scale = v_col * area
            f = []
            for s in (DIAG, ACROSS, DOWN):
                coded = frecv[part, s, :, cols].astype(jnp.int32).astype(F32)
                code = coded[vars_:vars_ + 1]
                f.append(coded[:vars_] * ((code * code) * (1.0 / (4096.0 * TOP))))
            f.append(fown[part, :, cols])
            goal = tgt[:, first:first + LANES] - b_col
            pairs = [None] * members
            spread = jnp.zeros((vars_, LANES), F32)
            for i in range(members):
                for j in range(i + 1, members):
                    d = f[i] - f[j]
                    q = d * d + eps
                    inv = lax.rsqrt(q)
                    slope = d * inv
                    spread += q * inv - DELTA
                    pairs[i] = slope if pairs[i] is None else pairs[i] + slope
                    pairs[j] = -slope if pairs[j] is None else pairs[j] - slope
            miss_sum = jnp.zeros((vars_, LANES), F32)
            for s in range(members):
                d = f[s] - goal
                q = d * d + eps
                inv = lax.rsqrt(q)
                miss_sum += q * inv - DELTA
                cot = scale * (d * inv - pairs[s] * (1.0 / (members - 1)))
                b_sum += cot
                if s == SELF:
                    crecv[part, SELF, :vars_, cols] = cot.astype(BF)
                else:
                    csend[part, s, :vars_, cols] = cot.astype(BF)
            l_sum += scale * (miss_sum - spread * (1.0 / (members - 1)))
        sums["b"], sums["l"] = b_sum, l_sum
        for s in (DIAG, ACROSS, DOWN):
            c_copies[part, s] = send(csend.at[part, s], crecv.at[part, s], member_dev(s))

    tgt_copy.wait()
    todo = [(part, s) for part in range(parts) for s in (DIAG, ACROSS, DOWN, SELF)]
    ready = activate(*todo[0])
    for n, (part, s) in enumerate(todo):
        project(part, s, ready)
        if n + 1 < len(todo):
            ready = activate(*todo[n + 1])
        send_field(part, s)
        if s == DOWN and part > 0:
            score(part - 1)
    score(parts - 1)
    lane_sums[:vars_, :] = sums["b"]
    sm[1:2, :LANES] = jnp.sum(lane_sums[...].T, axis=0, keepdims=True)
    sm[1:2, LANES:2 * LANES] = jnp.sum(sums["l"], axis=0, keepdims=True)

    col = jnp.zeros((1, latent), F32)
    for part in range(parts):
        for s in (SELF, ACROSS, DOWN, DIAG):
            if s == ACROSS:
                for k in (ACROSS, DOWN, DIAG):
                    c_copies[part, k].wait_recv()
            r0 = pl.multiple_of(mem[s] * sub + part * TILE, TILE)
            cot_b = crecv[part, s, :vars_]
            d = dot(cot_b, w_out[...], TN) * gp[pl.ds(r0, TILE), :]
            dpre[pl.ds(r0, TILE), :] = d.astype(BF)
            ot[:vars_, :] += dot(cot_b, act[pl.ds(r0, TILE), :], NN)
            col += jnp.sum(d, axis=0, keepdims=True)
    sm[0:1, :] = col

    share = ot.shape[0] // (2 * planes)
    first_half = pl.multiple_of(other * (planes * share), share)
    op_send[...] = ot[pl.ds(first_half, planes * share), :].astype(BF)
    op_copy = send(op_send, op_recv, partner)
    sp_copy = send(sm, sp_recv, partner)

    p_copies = {}
    d_copies = {}
    n_copies = {}
    far_half = 1 - z // 2
    halves = (far_half, z // 2)
    pairs_of = ((DIAG, ACROSS), (DOWN, SELF))

    def chunk(h, pair):
        n = h * 2 + pair
        lo = pair * 2
        left = lat_t[halves[h], lo:lo + 2].reshape(width, points)
        keep[...] = dot(left, dpre[...], NN).reshape(2, 2, 2, rows, latent)
        p_send[n] = keep[:, :, other].astype(BF)
        part_sum[h, lo:lo + 2] = keep[:, :, c]
        p_copies[n] = send(p_send.at[n], p_recv.at[n], partner)

    def fold(h, pair):
        n = h * 2 + pair
        p_copies[n].wait_recv()
        lo = pair * 2
        both = part_sum[h, lo:lo + 2] + p_recv[n].astype(F32)
        if pair == 0:
            d_send[h] = both[0].astype(BF)
            d_copies[h] = [
                send(d_send.at[h, j], d_recv.at[h, j], member_dev(ACROSS + j)) for j in range(2)
            ]
            n_send[h, 0, 0] = both[1, 0].astype(BF)
            part_sum[h, ACROSS, 1] = both[1, 1]
        else:
            n_send[h, 1, 1] = both[0, 1].astype(BF)
            part_sum[h, DOWN, 0] = both[0, 0]
            part_sum[h, SELF] = both[1]

    def direct(h, s):
        j = s - 1
        n_copies[h, s, j] = send(n_send.at[h, j, j], n_recv.at[h, j, j], member_dev(s))

    def relay_sum(h):
        for s, j in ((DOWN, 0), (ACROSS, 1)):
            d_copies[h][j].wait_recv()
            n_send[h, s - 1, j] = (part_sum[h, s, j] + d_recv[h, j].astype(F32)).astype(BF)
            n_copies[h, s, j] = send(n_send.at[h, s - 1, j], n_recv.at[h, s - 1, j], member_dev(s))

    def plane_sum(h):
        for s in (ACROSS, DOWN):
            for j in range(2):
                n_copies[h, s, j].wait_recv()
        part_sum[h, SELF] = (part_sum[h, SELF] + n_recv[h, 0].astype(F32)) + n_recv[h, 1].astype(F32)

    side = lax.rem(z, 2)
    zz_copies = []

    def to_plane(n, value, k):
        z_send[n] = value.astype(BF)
        zz_copies.append(send(z_send.at[n], z_recv.at[n], z_dev(k)))

    def hidden_grad(ch):
        w = w_buf[ch].reshape(width, latent)
        gh[0, :, ch * width:(ch + 1) * width] = dot(dpre[...], w, NT).astype(BF)

    def open_out():
        op_copy.wait_recv()
        mine = pl.multiple_of(c * (planes * share), share)
        om[...] = (ot[pl.ds(mine, planes * share), :] + op_recv[...].astype(F32)).reshape(planes, share, latent)
        om_send[...] = om[...].astype(BF)
        return [send(om_send.at[zed[k]], om_recv.at[k - 1], z_dev(k)) for k in range(1, planes)]

    def cross_out():
        acc = om[z]
        for k in range(1, planes):
            om_copies[k - 1].wait_recv()
            acc += om_recv[k - 1].astype(F32)
        oq[m] = acc.astype(BF)
        return [send(oq.at[m], oq.at[m], member_dev(s)) for s in (DIAG, ACROSS, DOWN)]

    def close_out():
        for copy in oq_copies:
            copy.wait_recv()
        acc = oq[0].astype(F32)
        for k in range(1, members):
            acc += oq[k].astype(F32)
        w2[c, z] = acc.astype(BF)
        return [send(w2.at[c, z], w2.at[c, z], z_dev(k)) for k in range(1, planes)]

    chunk(0, 0)
    om_copies = open_out()
    sp_copy.wait_recv()
    smm[m] = sm[...] + sp_recv[...]
    sm_copies = [send(smm.at[m], smm.at[m], member_dev(s)) for s in (DIAG, ACROSS, DOWN)]
    chunk(0, 1)
    fold(0, 0)
    direct(0, ACROSS)
    chunk(1, 0)
    fold(0, 1)
    direct(0, DOWN)
    chunk(1, 1)
    oq_copies = cross_out()
    relay_sum(0)
    hidden_grad(0)
    fold(1, 0)
    direct(1, ACROSS)
    fold(1, 1)
    direct(1, DOWN)
    for copy in sm_copies:
        copy.wait_recv()
    acc = smm[0]
    for k in range(1, members):
        acc += smm[k]
    smz[z] = acc
    sz_copies = [send(smz.at[z], smz.at[z], z_dev(k)) for k in range(1, planes)]
    w2_copies = close_out()
    hidden_grad(1)
    plane_sum(0)
    to_plane(0, part_sum[0, SELF, 1 - side], 1)
    hidden_grad(2)
    relay_sum(1)
    zz_copies[0].wait_recv()
    to_plane(1, part_sum[0, SELF, side] + z_recv[0].astype(F32), 2)
    hidden_grad(3)
    for copy in w2_copies:
        copy.wait_recv()
    half_copy = send(w2.at[c], w2.at[c], partner)
    plane_sum(1)
    to_plane(2, part_sum[1, SELF, 1 - side], 1)
    acc = part_sum[1, SELF, side]

    kappa = 4.0 / math.sqrt(members * total)
    for copy in sz_copies:
        copy.wait_recv()
    small = smz[0]
    for k in range(1, planes):
        small += smz[k]
    small = small * kappa
    g_b1[...] = small[0:1, :]
    g_b2[...] = small[1:2, :vars_]
    g_loss[...] = jnp.sum(small[1:2, LANES:2 * LANES], axis=1, keepdims=True) * (1.0 / (kappa * members * total * vars_))
    half_copy.wait_recv()
    g_w2[...] = w2[...].reshape(2 * planes * share, latent)[:vars_].astype(F32) * kappa
    for n in (1, 2):
        zz_copies[n].wait_recv()
        acc += z_recv[n].astype(F32)
    g_w1[...] = acc * kappa
    for copy in started:
        copy.wait_send()


def store_kernel(*refs):
    count = len(refs) // 2
    copies = []
    for n in range(count):
        copy = pltpu.make_async_copy(refs[n], refs[count + n], refs[2 * count].at[n])
        copy.start()
        copies.append(copy)
    for copy in copies:
        copy.wait()


def fast(latent, w_in, b_in, w_out, b_out, targets, var_weight, plan):
    members = lax.axis_size("member")
    grid = lax.axis_size("grid")
    planes = grid // 2
    points, width = latent.shape[1], latent.shape[2]
    rows = w_in.shape[0]
    vars_ = w_out.shape[0]
    sub = points // members
    cw = width // members
    parts = sub // TILE
    share = 16 * pl.cdiv(vars_, 32 * planes)
    pad = 8 * pl.cdiv(vars_ + 1, 8)
    n_sems = (planes - 1) * 4 + planes * 10 + (members - 1) * (4 + 2 * parts) + 2 * members + 24
    vmem = pl.BlockSpec(memory_space=pltpu.VMEM)
    hbm = pl.BlockSpec(memory_space=pl.ANY)
    V = pltpu.VMEM
    block = (rows, width)
    scratch = [
        V((members, points, cw), BF), V((2, members, cw // 2, points), BF), V((members, planes, 2, *block), BF),
        V((points, width), F32), V((points, width), BF), V((points, width), BF),
        V((1, width), F32), V((vars_, width), BF), V((1, vars_), F32), V((1, vars_), F32),
        V((pad, width), BF), V((parts, vars_, TILE), F32),
        V((parts, members - 1, pad, TILE), I16), V((parts, members - 1, pad, TILE), I16),
        V((parts, members - 1, pad, TILE), BF), V((parts, members, pad, TILE), BF), V((vars_, sub), F32),
        V((8, LANES), F32), V((LANES, LANES), F32),
        V((2 * planes * share, width), F32), V((planes * share, width), BF), V((planes * share, width), BF),
        V((planes, share, width), F32), V((planes, share, width), BF), V((planes - 1, share, width), BF),
        V((members, share, width), BF), V((2, planes, share, width), BF),
        V((2, width), F32), V((2, width), F32), V((members, 2, width), F32), V((planes, 2, width), F32),
        V((2, 2, 2, *block), F32), V((2, members, 2, *block), F32),
        V((4, 2, 2, *block), BF), V((4, 2, 2, *block), BF),
        V((2, 2, *block), BF), V((2, 2, *block), BF), V((2, 2, 2, *block), BF), V((2, 2, 2, *block), BF),
        V((planes - 1, *block), BF), V((planes - 1, *block), BF),
        pltpu.SemaphoreType.DMA((n_sems,)), pltpu.SemaphoreType.DMA((n_sems,)),
        pltpu.SemaphoreType.DMA((members + 6,)),
    ]
    S = jax.ShapeDtypeStruct
    shapes = [
        ((1, points, width), BF), ((rows, width), F32), ((1, width), F32),
        ((vars_, width), F32), ((1, vars_), F32), ((1, 1), F32),
    ]
    held = pl.pallas_call(
        functools.partial(head_kernel, members, planes),
        out_shape=[pltpu.VMEM(*s) for s in shapes],
        in_specs=[hbm] * 7,
        out_specs=[vmem] * len(shapes),
        scratch_shapes=scratch,
        compiler_params=pltpu.CompilerParams(
            collective_id=0, has_side_effects=True, vmem_limit_bytes=57000 * 1024
        ),
    )(latent, w_in, b_in[None], w_out, b_out[None], targets, var_weight[None])
    gh, g_w1, g_b1, g_w2, g_b2, g_loss = pl.pallas_call(
        store_kernel,
        out_shape=[S(*s) for s in shapes],
        in_specs=[hbm] * len(shapes),
        out_specs=[hbm] * len(shapes),
        scratch_shapes=[pltpu.SemaphoreType.DMA((len(shapes),))],
        compiler_params=pltpu.CompilerParams(has_side_effects=True, vmem_limit_bytes=1024 * 1024),
    )(*[pltpu.with_memory_space_constraint(h, pltpu.VMEM) for h in held])
    return g_loss[0, 0], gh, g_w1, g_b1[0], g_w2, g_b2[0]


def local(latent, w_in, b_in, w_out, b_out, targets, var_weight, plan):
    members = lax.axis_size("member")
    grid = lax.axis_size("grid")
    points, width = latent.shape[1], latent.shape[2]
    whole_plan = plan.shape[0] == members - 1
    tiled = (
        w_in.shape[0] % 16 == 0 and grid == 8 and members == 4
        and points % (members * TILE) == 0 and width % (2 * members * LANES) == 0
        and width // members == grid * w_in.shape[0] and w_out.shape[0] < LANES
        and points * width <= 2048 * 1024
    )
    run = fast if whole_plan and tiled else shards
    return run(latent, w_in, b_in, w_out, b_out, targets, var_weight, plan)


def solution(mesh):
    placed = (
        P("member", "grid", None),
        P(("member", "grid"), None),
        P(),
        P(),
        P(),
        P(None, "grid"),
        P(),
        P(),
    )
    return jax.shard_map(
        local,
        mesh=mesh,
        in_specs=placed,
        out_specs=(P(), P("member", "grid", None), P(("member", "grid"), None), P(), P(), P()),
        check_vma=False,
    )
```

```python
import functools
import math

import jax
import jax.numpy as jnp
from jax import lax
from jax.experimental import pallas as pl
from jax.experimental.pallas import tpu as pltpu
from jax.sharding import PartitionSpec as P

DELTA = 0.25


def make_fold(mine, partner_rows):

    def fold(carry, piece, start):
        count = piece.shape[0]
        labels = jnp.arange(count, dtype=jnp.int32)
        weights = jnp.sum((partner_rows[:, None] == labels[None, :]).astype(jnp.float32), axis=0)
        diff = mine[None] - piece
        root = jnp.sqrt(diff * diff + DELTA * DELTA)
        slope_sum = jnp.einsum("k,kvp->vp", weights, diff / root)
        spread_sum = jnp.einsum("k,kvp->vp", weights, root - DELTA)
        return (slope_sum, spread_sum)

    return fold


def shards(latent, w_in, b_in, w_out, b_out, targets, var_weight, plan):
    hidden_in = latent[0]
    points = hidden_in.shape[0]
    rounds = plan.shape[0]
    w_full = lax.all_gather(w_in, ("member", "grid"), axis=0, tiled=True)
    member = lax.axis_index("member")
    grid_index = lax.axis_index("grid")
    members = lax.axis_size("member")
    grid_count = lax.axis_size("grid")
    total = points * grid_count
    place = (grid_index * points + jnp.arange(points, dtype=jnp.int32)).astype(jnp.float32)
    area = jnp.cos(1.4 * (place + 0.5) / total)
    scale_map = area[None, :] * var_weight[:, None]
    partner_rows = lax.dynamic_index_in_dim(plan, member, 1, keepdims=False)
    pre = jnp.dot(hidden_in, w_full, preferred_element_type=jnp.float32) + b_in[None, :]
    act = jax.nn.gelu(pre).astype(jnp.bfloat16)
    field = jnp.dot(w_out, act.T, preferred_element_type=jnp.float32) + b_out[:, None]
    pre, act, field = (pre, act, field)
    fold_all = make_fold(field, partner_rows)
    slope_sum, spread_sum = fold_all(
        (
            jnp.zeros((w_out.shape[0], points), jnp.float32),
            jnp.zeros((w_out.shape[0], points), jnp.float32),
        ),
        lax.all_gather(field[None], "member", axis=0, tiled=True),
        jnp.int32(0),
    )
    miss = field - targets
    miss_root = jnp.sqrt(miss * miss + DELTA * DELTA)
    cot = scale_map * (miss / miss_root - slope_sum / rounds)
    terms = scale_map * (miss_root - DELTA - spread_sum / (2.0 * rounds))
    cot_b = cot.astype(jnp.bfloat16)
    dact = jnp.dot(cot_b.T, w_out, preferred_element_type=jnp.float32)
    _, pull = jax.vjp(jax.nn.gelu, pre)
    dpre = pull(dact)[0]
    dpre_b = dpre.astype(jnp.bfloat16)
    grad_hidden = jnp.dot(dpre_b, w_full.T, preferred_element_type=jnp.float32).astype(jnp.bfloat16)
    kappa = 4.0 / jnp.sqrt(jnp.float32(members * total))
    out_term = jnp.dot(cot_b, act, preferred_element_type=jnp.float32)
    sum_w2, sum_b2, sum_b1, sum_loss = lax.psum(
        (out_term, jnp.sum(cot, axis=1), jnp.sum(dpre, axis=0), jnp.sum(terms)), ("member", "grid")
    )
    row_count = w_in.shape[0]
    full_term = jnp.dot(hidden_in.T, dpre_b, preferred_element_type=jnp.float32)
    summed = lax.psum(full_term, ("member", "grid"))
    offset = (member * grid_count + grid_index) * row_count
    own_rows = lax.dynamic_slice_in_dim(summed, offset, row_count, 0)
    loss = sum_loss / (members * total * w_out.shape[0])
    return (
        loss,
        grad_hidden[None],
        own_rows * kappa,
        sum_b1 * kappa,
        sum_w2 * kappa,
        sum_b2 * kappa,
    )


TILE = 256
LANES = 128
BF = jnp.bfloat16
F32 = jnp.float32
I16 = jnp.int16
TOP = 32767.0
DIAG, ACROSS, DOWN, SELF = 0, 1, 2, 3


def dot(a, b, dims):
    return lax.dot_general(a, b, (dims, ((), ())), preferred_element_type=F32)


NN = ((1,), (0,))
NT = ((1,), (1,))
TN = ((0,), (0,))


def head_kernel(
    members, planes, lat_hbm, w_in, b_in_hbm, w_out_hbm, b_out_hbm, tgt_hbm, vw_hbm,
    gh, g_w1, g_b1, g_w2, g_b2, g_loss,
    lat, lat_t, w_buf, gp, act, dpre, b_in, w_out, b_out, vw, wo, fown, fsend, frecv, csend, crecv, tgt, rowbuf, lane_sums,
    ot, op_send, op_recv, om, om_send, om_recv, oq, w2, sm, sp_recv, smm, smz,
    keep, part_sum, p_send, p_recv, d_send, d_recv, n_send, n_recv, z_send, z_recv,
    send_sem, recv_sem, local_sem,
):
    m = lax.axis_index("member")
    g = lax.axis_index("grid")
    z, c = g // 2, lax.rem(g, 2)
    other = 1 - c
    points = lat.shape[1]
    width = lat.shape[2]
    sub = points // members
    rows = w_in.shape[0]
    vars_ = w_out.shape[0]
    pad = wo.shape[0]
    latent = w_out.shape[1]
    total = points * planes * 2
    half = width // 2

    mem = (members - 1 - m, m + 1 - 2 * lax.rem(m, 2), m + 2 - 4 * (m // 2), m)
    zed = (z, z + 1 - 2 * lax.rem(z, 2), z + 2 - 4 * (z // 2), planes - 1 - z)

    partner = (m, z * 2 + other)

    def member_dev(s):
        return (mem[s], g)

    def z_dev(k):
        return (m, zed[k] * 2 + c)

    started = []

    def send(src, dst, dev):
        n = len(started)
        copy = pltpu.make_async_remote_copy(
            src_ref=src, dst_ref=dst, send_sem=send_sem.at[n], recv_sem=recv_sem.at[n],
            device_id=dev, device_id_type=pl.DeviceIdType.MESH,
        )
        copy.start()
        started.append(copy)
        return copy

    barrier = pltpu.get_barrier_semaphore()
    peers = [partner] + [z_dev(k) for k in range(1, planes)] + [member_dev(s) for s in (DIAG, ACROSS, DOWN)]
    for dev in peers:
        pl.semaphore_signal(barrier, inc=1, device_id=dev, device_id_type=pl.DeviceIdType.MESH)
    pl.semaphore_wait(barrier, len(peers))

    near = {ACROSS: [], DOWN: []}
    far = []
    to_part = {s: [] for s in range(members)}
    z_copies = [None]

    def block(s, step):
        return w_buf.at[mem[s], zed[step], c]

    def hand_over(s, step):
        to_part[s].append(send(block(s, step), block(s, step), partner))

    def spread_block(step):
        if step > 0:
            z_copies[step].wait_recv()
        if step == 2:
            z_copies.append(send(block(SELF, 2), block(SELF, 2), z_dev(1)))
        src = w_in if step == 0 else block(SELF, step)
        for s in (ACROSS, DOWN):
            near[s].append(send(src, block(SELF, step), member_dev(s)))
        to_part[SELF].append(send(src, block(SELF, step), partner))

    def relay_block(step):
        for s in (ACROSS, DOWN):
            near[s][step].wait_recv()
        s = ACROSS if step % 2 == 0 else DOWN
        far.append(send(block(s, step), block(s, step), member_dev(ACROSS + DOWN - s)))
        hand_over(ACROSS, step)
        hand_over(DOWN, step)

    def far_block(step):
        far[step].wait_recv()
        hand_over(DIAG, step)

    def transpose_next():
        s, copy = loads.pop(0)
        copy.wait()

        def body(t, carry):
            r0 = pl.multiple_of(t * 2 * TILE, 2 * TILE)
            turned = lat[s, pl.ds(r0, 2 * TILE), :].T
            lat_t[0, s, :, pl.ds(r0, 2 * TILE)] = turned[:half]
            lat_t[1, s, :, pl.ds(r0, 2 * TILE)] = turned[half:]
            return carry

        lax.fori_loop(0, points // (2 * TILE), body, 0)

    def contract(slots, first):
        for s in slots:
            for copy in to_part[s]:
                copy.wait_recv()
        big = 4 * TILE

        def body(t, carry):
            r0 = pl.multiple_of(t * big, big)
            acc = b_in[...] if first else gp[pl.ds(r0, big), :]
            for s in slots:
                acc = acc + dot(lat[s, pl.ds(r0, big), :], w_buf[mem[s]].reshape(width, latent), NN)
            gp[pl.ds(r0, big), :] = acc
            return carry

        lax.fori_loop(0, points // big, body, 0)

    z_copies.append(send(w_in, w_buf.at[m, z, c], z_dev(1)))
    z_copies.append(send(w_in, w_buf.at[m, z, c], z_dev(2)))
    spread_block(0)

    own = pltpu.make_async_copy(w_in, w_buf.at[m, z, c], local_sem.at[members])
    own.start()
    loads = []
    for s in (SELF, ACROSS, DOWN, DIAG):
        copy = pltpu.make_async_copy(
            lat_hbm.at[0, :, pl.ds(pl.multiple_of(mem[s] * width, LANES), width)], lat.at[s], local_sem.at[s]
        )
        copy.start()
        loads.append((s, copy))
    tgt_copy = pltpu.make_async_copy(
        tgt_hbm.at[:, pl.ds(pl.multiple_of(m * sub, LANES), sub)], tgt, local_sem.at[members + 1]
    )
    tgt_copy.start()
    small_copies = []
    for n, (src, dst) in enumerate(((b_out_hbm, b_out), (vw_hbm, vw), (w_out_hbm, w_out), (b_in_hbm, b_in))):
        copy = pltpu.make_async_copy(src, dst, local_sem.at[members + 2 + n])
        copy.start()
        small_copies.append(copy)


    wo[...] = jnp.zeros_like(wo)
    for copy in small_copies:
        copy.wait()
    wo[:vars_, :] = w_out[...]
    rowbuf[...] = jnp.zeros_like(rowbuf)
    rowbuf[0:1, :vars_] = b_out[...]
    rowbuf[1:2, :vars_] = vw[...]
    b_col = jnp.broadcast_to(rowbuf[0:1, :], (LANES, LANES)).T[:vars_]
    v_col = jnp.broadcast_to(rowbuf[1:2, :], (LANES, LANES)).T[:vars_]
    lane_sums[...] = jnp.zeros_like(lane_sums)
    ot[...] = jnp.zeros_like(ot)
    sm[...] = jnp.zeros_like(sm)
    csend[...] = jnp.zeros_like(csend)
    own.wait()

    transpose_next()
    relay_block(0)
    spread_block(1)
    transpose_next()
    spread_block(2)
    relay_block(1)
    transpose_next()
    spread_block(3)
    relay_block(2)
    far_block(0)
    transpose_next()
    contract((SELF,), True)
    relay_block(3)
    far_block(1)
    far_block(2)
    contract((ACROSS, DOWN), False)
    far_block(3)
    for copy in to_part[DIAG]:
        copy.wait_recv()

    c0 = math.sqrt(2.0 / math.pi)
    parts = sub // TILE
    f_copies = {}
    eps = DELTA * DELTA
    c_copies = {}
    sums = {"b": jnp.zeros((vars_, LANES), F32), "l": jnp.zeros((vars_, LANES), F32)}

    def activate(part, s):
        r0 = pl.multiple_of(mem[s] * sub + part * TILE, TILE)
        x = dot(lat[DIAG, pl.ds(r0, TILE), :], w_buf[mem[DIAG]].reshape(width, latent), NN)
        x = x + gp[pl.ds(r0, TILE), :]
        sq = x * x
        cdf = 0.5 + 0.5 * jnp.tanh(x * (c0 + (0.044715 * c0) * sq))
        out = x * cdf
        rounded = out.astype(BF)
        act[pl.ds(r0, TILE), :] = rounded
        gp[pl.ds(r0, TILE), :] = cdf + (out * (1.0 - cdf)) * (2.0 * c0 + (6.0 * 0.044715 * c0) * sq)
        return rounded

    def project(part, s, rounded):
        field = dot(wo[...], rounded, NT)
        if s == SELF:
            fown[part] = field[:vars_]
        else:
            peak = jnp.max(jnp.abs(field), axis=0, keepdims=True)
            code = jnp.floor(jnp.sqrt(peak) * 64.0) + 2.0
            scale = (code * code) * (1.0 / 4096.0)
            coded = jnp.round(field * (TOP / scale))
            at = lax.broadcasted_iota(jnp.int32, (pad, TILE), 0)
            coded = jnp.where(at == vars_, jnp.broadcast_to(code, (pad, TILE)), coded)
            fsend[part, s] = coded.astype(jnp.int32).astype(I16)

    def send_field(part, s):
        if s != SELF:
            f_copies[part, s] = send(fsend.at[part, s], frecv.at[part, s], member_dev(s))

    def score(part):
        for s in (DIAG, ACROSS, DOWN):
            f_copies[part, s].wait_recv()
        b_sum, l_sum = sums["b"], sums["l"]
        for at in range(TILE // LANES):
            cols = slice(at * LANES, (at + 1) * LANES)
            first = part * TILE + at * LANES
            place = lax.broadcasted_iota(jnp.int32, (1, LANES), 1) + (g * points + m * sub + first)
            area = jnp.cos(1.4 * (place.astype(F32) + 0.5) / total)
            scale = v_col * area
            f = []
            for s in (DIAG, ACROSS, DOWN):
                coded = frecv[part, s, :, cols].astype(jnp.int32).astype(F32)
                code = coded[vars_:vars_ + 1]
                f.append(coded[:vars_] * ((code * code) * (1.0 / (4096.0 * TOP))))
            f.append(fown[part, :, cols])
            goal = tgt[:, first:first + LANES] - b_col
            pairs = [None] * members
            spread = jnp.zeros((vars_, LANES), F32)
            for i in range(members):
                for j in range(i + 1, members):
                    d = f[i] - f[j]
                    q = d * d + eps
                    inv = lax.rsqrt(q)
                    slope = d * inv
                    spread += q * inv - DELTA
                    pairs[i] = slope if pairs[i] is None else pairs[i] + slope
                    pairs[j] = -slope if pairs[j] is None else pairs[j] - slope
            miss_sum = jnp.zeros((vars_, LANES), F32)
            for s in range(members):
                d = f[s] - goal
                q = d * d + eps
                inv = lax.rsqrt(q)
                miss_sum += q * inv - DELTA
                cot = scale * (d * inv - pairs[s] * (1.0 / (members - 1)))
                b_sum += cot
                if s == SELF:
                    crecv[part, SELF, :vars_, cols] = cot.astype(BF)
                else:
                    csend[part, s, :vars_, cols] = cot.astype(BF)
            l_sum += scale * (miss_sum - spread * (1.0 / (members - 1)))
        sums["b"], sums["l"] = b_sum, l_sum
        for s in (DIAG, ACROSS, DOWN):
            c_copies[part, s] = send(csend.at[part, s], crecv.at[part, s], member_dev(s))

    tgt_copy.wait()
    todo = [(part, s) for part in range(parts) for s in (DIAG, ACROSS, DOWN, SELF)]
    ready = activate(*todo[0])
    for n, (part, s) in enumerate(todo):
        project(part, s, ready)
        if n + 1 < len(todo):
            ready = activate(*todo[n + 1])
        send_field(part, s)
        if s == DOWN and part > 0:
            score(part - 1)
    score(parts - 1)
    lane_sums[:vars_, :] = sums["b"]
    sm[1:2, :LANES] = jnp.sum(lane_sums[...].T, axis=0, keepdims=True)
    sm[1:2, LANES:2 * LANES] = jnp.sum(sums["l"], axis=0, keepdims=True)

    col = jnp.zeros((1, latent), F32)
    for part in range(parts):
        for s in (SELF, ACROSS, DOWN, DIAG):
            if s == ACROSS:
                for k in (ACROSS, DOWN, DIAG):
                    c_copies[part, k].wait_recv()
            r0 = pl.multiple_of(mem[s] * sub + part * TILE, TILE)
            cot_b = crecv[part, s, :vars_]
            d = dot(cot_b, w_out[...], TN) * gp[pl.ds(r0, TILE), :]
            dpre[pl.ds(r0, TILE), :] = d.astype(BF)
            ot[:vars_, :] += dot(cot_b, act[pl.ds(r0, TILE), :], NN)
            col += jnp.sum(d, axis=0, keepdims=True)
    sm[0:1, :] = col

    share = ot.shape[0] // (2 * planes)
    first_half = pl.multiple_of(other * (planes * share), share)
    op_send[...] = ot[pl.ds(first_half, planes * share), :].astype(BF)
    op_copy = send(op_send, op_recv, partner)
    sp_copy = send(sm, sp_recv, partner)

    p_copies = {}
    d_copies = {}
    n_copies = {}
    far_half = 1 - z // 2
    halves = (far_half, z // 2)
    pairs_of = ((DIAG, ACROSS), (DOWN, SELF))

    def chunk(h, pair):
        n = h * 2 + pair
        lo = pair * 2
        left = lat_t[halves[h], lo:lo + 2].reshape(width, points)
        keep[...] = dot(left, dpre[...], NN).reshape(2, 2, 2, rows, latent)
        p_send[n] = keep[:, :, other].astype(BF)
        part_sum[h, lo:lo + 2] = keep[:, :, c]
        p_copies[n] = send(p_send.at[n], p_recv.at[n], partner)

    def fold(h, pair):
        n = h * 2 + pair
        p_copies[n].wait_recv()
        lo = pair * 2
        both = part_sum[h, lo:lo + 2] + p_recv[n].astype(F32)
        if pair == 0:
            d_send[h] = both[0].astype(BF)
            d_copies[h] = [
                send(d_send.at[h, j], d_recv.at[h, j], member_dev(ACROSS + j)) for j in range(2)
            ]
            n_send[h, 0, 0] = both[1, 0].astype(BF)
            part_sum[h, ACROSS, 1] = both[1, 1]
        else:
            n_send[h, 1, 1] = both[0, 1].astype(BF)
            part_sum[h, DOWN, 0] = both[0, 0]
            part_sum[h, SELF] = both[1]

    def direct(h, s):
        j = s - 1
        n_copies[h, s, j] = send(n_send.at[h, j, j], n_recv.at[h, j, j], member_dev(s))

    def relay_sum(h):
        for s, j in ((DOWN, 0), (ACROSS, 1)):
            d_copies[h][j].wait_recv()
            n_send[h, s - 1, j] = (part_sum[h, s, j] + d_recv[h, j].astype(F32)).astype(BF)
            n_copies[h, s, j] = send(n_send.at[h, s - 1, j], n_recv.at[h, s - 1, j], member_dev(s))

    def plane_sum(h):
        for s in (ACROSS, DOWN):
            for j in range(2):
                n_copies[h, s, j].wait_recv()
        part_sum[h, SELF] = (part_sum[h, SELF] + n_recv[h, 0].astype(F32)) + n_recv[h, 1].astype(F32)

    side = lax.rem(z, 2)
    zz_copies = []

    def to_plane(n, value, k):
        z_send[n] = value.astype(BF)
        zz_copies.append(send(z_send.at[n], z_recv.at[n], z_dev(k)))

    def hidden_grad(ch):
        w = w_buf[ch].reshape(width, latent)
        gh[0, :, ch * width:(ch + 1) * width] = dot(dpre[...], w, NT).astype(BF)

    def open_out():
        op_copy.wait_recv()
        mine = pl.multiple_of(c * (planes * share), share)
        om[...] = (ot[pl.ds(mine, planes * share), :] + op_recv[...].astype(F32)).reshape(planes, share, latent)
        om_send[...] = om[...].astype(BF)
        return [send(om_send.at[zed[k]], om_recv.at[k - 1], z_dev(k)) for k in range(1, planes)]

    def cross_out():
        acc = om[z]
        for k in range(1, planes):
            om_copies[k - 1].wait_recv()
            acc += om_recv[k - 1].astype(F32)
        oq[m] = acc.astype(BF)
        return [send(oq.at[m], oq.at[m], member_dev(s)) for s in (DIAG, ACROSS, DOWN)]

    def close_out():
        for copy in oq_copies:
            copy.wait_recv()
        acc = oq[0].astype(F32)
        for k in range(1, members):
            acc += oq[k].astype(F32)
        w2[c, z] = acc.astype(BF)
        return [send(w2.at[c, z], w2.at[c, z], z_dev(k)) for k in range(1, planes)]

    chunk(0, 0)
    om_copies = open_out()
    sp_copy.wait_recv()
    smm[m] = sm[...] + sp_recv[...]
    sm_copies = [send(smm.at[m], smm.at[m], member_dev(s)) for s in (DIAG, ACROSS, DOWN)]
    chunk(0, 1)
    fold(0, 0)
    direct(0, ACROSS)
    chunk(1, 0)
    fold(0, 1)
    direct(0, DOWN)
    chunk(1, 1)
    oq_copies = cross_out()
    relay_sum(0)
    hidden_grad(0)
    fold(1, 0)
    direct(1, ACROSS)
    fold(1, 1)
    direct(1, DOWN)
    for copy in sm_copies:
        copy.wait_recv()
    acc = smm[0]
    for k in range(1, members):
        acc += smm[k]
    smz[z] = acc
    sz_copies = [send(smz.at[z], smz.at[z], z_dev(k)) for k in range(1, planes)]
    w2_copies = close_out()
    hidden_grad(1)
    plane_sum(0)
    to_plane(0, part_sum[0, SELF, 1 - side], 1)
    relay_sum(1)
    hidden_grad(2)
    zz_copies[0].wait_recv()
    to_plane(1, part_sum[0, SELF, side] + z_recv[0].astype(F32), 2)
    for copy in w2_copies:
        copy.wait_recv()
    half_copy = send(w2.at[c], w2.at[c], partner)
    plane_sum(1)
    to_plane(2, part_sum[1, SELF, 1 - side], 1)
    hidden_grad(3)
    acc = part_sum[1, SELF, side]

    kappa = 4.0 / math.sqrt(members * total)
    for copy in sz_copies:
        copy.wait_recv()
    small = smz[0]
    for k in range(1, planes):
        small += smz[k]
    small = small * kappa
    g_b1[...] = small[0:1, :]
    g_b2[...] = small[1:2, :vars_]
    g_loss[...] = jnp.sum(small[1:2, LANES:2 * LANES], axis=1, keepdims=True) * (1.0 / (kappa * members * total * vars_))
    half_copy.wait_recv()
    g_w2[...] = w2[...].reshape(2 * planes * share, latent)[:vars_].astype(F32) * kappa
    for n in (1, 2):
        zz_copies[n].wait_recv()
        acc += z_recv[n].astype(F32)
    g_w1[...] = acc * kappa
    for copy in started:
        copy.wait_send()


def store_kernel(*refs):
    count = len(refs) // 2
    copies = []
    for n in range(count):
        copy = pltpu.make_async_copy(refs[n], refs[count + n], refs[2 * count].at[n])
        copy.start()
        copies.append(copy)
    for copy in copies:
        copy.wait()


def fast(latent, w_in, b_in, w_out, b_out, targets, var_weight, plan):
    members = lax.axis_size("member")
    grid = lax.axis_size("grid")
    planes = grid // 2
    points, width = latent.shape[1], latent.shape[2]
    rows = w_in.shape[0]
    vars_ = w_out.shape[0]
    sub = points // members
    cw = width // members
    parts = sub // TILE
    share = 16 * pl.cdiv(vars_, 32 * planes)
    pad = 8 * pl.cdiv(vars_ + 1, 8)
    n_sems = (planes - 1) * 4 + planes * 10 + (members - 1) * (4 + 2 * parts) + 2 * members + 24
    vmem = pl.BlockSpec(memory_space=pltpu.VMEM)
    hbm = pl.BlockSpec(memory_space=pl.ANY)
    V = pltpu.VMEM
    block = (rows, width)
    scratch = [
        V((members, points, cw), BF), V((2, members, cw // 2, points), BF), V((members, planes, 2, *block), BF),
        V((points, width), F32), V((points, width), BF), V((points, width), BF),
        V((1, width), F32), V((vars_, width), BF), V((1, vars_), F32), V((1, vars_), F32),
        V((pad, width), BF), V((parts, vars_, TILE), F32),
        V((parts, members - 1, pad, TILE), I16), V((parts, members - 1, pad, TILE), I16),
        V((parts, members - 1, pad, TILE), BF), V((parts, members, pad, TILE), BF), V((vars_, sub), F32),
        V((8, LANES), F32), V((LANES, LANES), F32),
        V((2 * planes * share, width), F32), V((planes * share, width), BF), V((planes * share, width), BF),
        V((planes, share, width), F32), V((planes, share, width), BF), V((planes - 1, share, width), BF),
        V((members, share, width), BF), V((2, planes, share, width), BF),
        V((2, width), F32), V((2, width), F32), V((members, 2, width), F32), V((planes, 2, width), F32),
        V((2, 2, 2, *block), F32), V((2, members, 2, *block), F32),
        V((4, 2, 2, *block), BF), V((4, 2, 2, *block), BF),
        V((2, 2, *block), BF), V((2, 2, *block), BF), V((2, 2, 2, *block), BF), V((2, 2, 2, *block), BF),
        V((planes - 1, *block), BF), V((planes - 1, *block), BF),
        pltpu.SemaphoreType.DMA((n_sems,)), pltpu.SemaphoreType.DMA((n_sems,)),
        pltpu.SemaphoreType.DMA((members + 6,)),
    ]
    S = jax.ShapeDtypeStruct
    shapes = [
        ((1, points, width), BF), ((rows, width), F32), ((1, width), F32),
        ((vars_, width), F32), ((1, vars_), F32), ((1, 1), F32),
    ]
    held = pl.pallas_call(
        functools.partial(head_kernel, members, planes),
        out_shape=[pltpu.VMEM(*s) for s in shapes],
        in_specs=[hbm] * 7,
        out_specs=[vmem] * len(shapes),
        scratch_shapes=scratch,
        compiler_params=pltpu.CompilerParams(
            collective_id=0, has_side_effects=True, vmem_limit_bytes=57000 * 1024
        ),
    )(latent, w_in, b_in[None], w_out, b_out[None], targets, var_weight[None])
    gh, g_w1, g_b1, g_w2, g_b2, g_loss = pl.pallas_call(
        store_kernel,
        out_shape=[S(*s) for s in shapes],
        in_specs=[hbm] * len(shapes),
        out_specs=[hbm] * len(shapes),
        scratch_shapes=[pltpu.SemaphoreType.DMA((len(shapes),))],
        compiler_params=pltpu.CompilerParams(has_side_effects=True, vmem_limit_bytes=1024 * 1024),
    )(*[pltpu.with_memory_space_constraint(h, pltpu.VMEM) for h in held])
    return g_loss[0, 0], gh, g_w1, g_b1[0], g_w2, g_b2[0]


def local(latent, w_in, b_in, w_out, b_out, targets, var_weight, plan):
    members = lax.axis_size("member")
    grid = lax.axis_size("grid")
    points, width = latent.shape[1], latent.shape[2]
    whole_plan = plan.shape[0] == members - 1
    tiled = (
        w_in.shape[0] % 16 == 0 and grid == 8 and members == 4
        and points % (members * TILE) == 0 and width % (2 * members * LANES) == 0
        and width // members == grid * w_in.shape[0] and w_out.shape[0] < LANES
        and points * width <= 2048 * 1024
    )
    run = fast if whole_plan and tiled else shards
    return run(latent, w_in, b_in, w_out, b_out, targets, var_weight, plan)


def solution(mesh):
    placed = (
        P("member", "grid", None),
        P(("member", "grid"), None),
        P(),
        P(),
        P(),
        P(None, "grid"),
        P(),
        P(),
    )
    return jax.shard_map(
        local,
        mesh=mesh,
        in_specs=placed,
        out_specs=(P(), P("member", "grid", None), P(("member", "grid"), None), P(), P(), P()),
        check_vma=False,
    )
```

```python
import functools
import math

import jax
import jax.numpy as jnp
from jax import lax
from jax.experimental import pallas as pl
from jax.experimental.pallas import tpu as pltpu
from jax.sharding import PartitionSpec as P

DELTA = 0.25


def make_fold(mine, partner_rows):

    def fold(carry, piece, start):
        count = piece.shape[0]
        labels = jnp.arange(count, dtype=jnp.int32)
        weights = jnp.sum((partner_rows[:, None] == labels[None, :]).astype(jnp.float32), axis=0)
        diff = mine[None] - piece
        root = jnp.sqrt(diff * diff + DELTA * DELTA)
        slope_sum = jnp.einsum("k,kvp->vp", weights, diff / root)
        spread_sum = jnp.einsum("k,kvp->vp", weights, root - DELTA)
        return (slope_sum, spread_sum)

    return fold


def shards(latent, w_in, b_in, w_out, b_out, targets, var_weight, plan):
    hidden_in = latent[0]
    points = hidden_in.shape[0]
    rounds = plan.shape[0]
    w_full = lax.all_gather(w_in, ("member", "grid"), axis=0, tiled=True)
    member = lax.axis_index("member")
    grid_index = lax.axis_index("grid")
    members = lax.axis_size("member")
    grid_count = lax.axis_size("grid")
    total = points * grid_count
    place = (grid_index * points + jnp.arange(points, dtype=jnp.int32)).astype(jnp.float32)
    area = jnp.cos(1.4 * (place + 0.5) / total)
    scale_map = area[None, :] * var_weight[:, None]
    partner_rows = lax.dynamic_index_in_dim(plan, member, 1, keepdims=False)
    pre = jnp.dot(hidden_in, w_full, preferred_element_type=jnp.float32) + b_in[None, :]
    act = jax.nn.gelu(pre).astype(jnp.bfloat16)
    field = jnp.dot(w_out, act.T, preferred_element_type=jnp.float32) + b_out[:, None]
    pre, act, field = (pre, act, field)
    fold_all = make_fold(field, partner_rows)
    slope_sum, spread_sum = fold_all(
        (
            jnp.zeros((w_out.shape[0], points), jnp.float32),
            jnp.zeros((w_out.shape[0], points), jnp.float32),
        ),
        lax.all_gather(field[None], "member", axis=0, tiled=True),
        jnp.int32(0),
    )
    miss = field - targets
    miss_root = jnp.sqrt(miss * miss + DELTA * DELTA)
    cot = scale_map * (miss / miss_root - slope_sum / rounds)
    terms = scale_map * (miss_root - DELTA - spread_sum / (2.0 * rounds))
    cot_b = cot.astype(jnp.bfloat16)
    dact = jnp.dot(cot_b.T, w_out, preferred_element_type=jnp.float32)
    _, pull = jax.vjp(jax.nn.gelu, pre)
    dpre = pull(dact)[0]
    dpre_b = dpre.astype(jnp.bfloat16)
    grad_hidden = jnp.dot(dpre_b, w_full.T, preferred_element_type=jnp.float32).astype(jnp.bfloat16)
    kappa = 4.0 / jnp.sqrt(jnp.float32(members * total))
    out_term = jnp.dot(cot_b, act, preferred_element_type=jnp.float32)
    sum_w2, sum_b2, sum_b1, sum_loss = lax.psum(
        (out_term, jnp.sum(cot, axis=1), jnp.sum(dpre, axis=0), jnp.sum(terms)), ("member", "grid")
    )
    row_count = w_in.shape[0]
    full_term = jnp.dot(hidden_in.T, dpre_b, preferred_element_type=jnp.float32)
    summed = lax.psum(full_term, ("member", "grid"))
    offset = (member * grid_count + grid_index) * row_count
    own_rows = lax.dynamic_slice_in_dim(summed, offset, row_count, 0)
    loss = sum_loss / (members * total * w_out.shape[0])
    return (
        loss,
        grad_hidden[None],
        own_rows * kappa,
        sum_b1 * kappa,
        sum_w2 * kappa,
        sum_b2 * kappa,
    )


TILE = 256
LANES = 128
BF = jnp.bfloat16
F32 = jnp.float32
I16 = jnp.int16
TOP = 32767.0
DIAG, ACROSS, DOWN, SELF = 0, 1, 2, 3


def dot(a, b, dims):
    return lax.dot_general(a, b, (dims, ((), ())), preferred_element_type=F32)


NN = ((1,), (0,))
NT = ((1,), (1,))
TN = ((0,), (0,))


def head_kernel(
    members, planes, lat_hbm, w_in, b_in_hbm, w_out_hbm, b_out_hbm, tgt_hbm, vw_hbm,
    gh, g_w1, g_b1, g_w2, g_b2, g_loss,
    lat, lat_t, w_buf, gp, act, dpre, b_in, w_out, b_out, vw, wo, fown, fsend, frecv, csend, crecv, tgt, rowbuf, lane_sums,
    ot, op_send, op_recv, om, om_send, om_recv, oq, w2, sm, sp_recv, smm, smz,
    keep, part_sum, p_send, p_recv, d_send, d_recv, n_send, n_recv, z_send, z_recv,
    send_sem, recv_sem, local_sem,
):
    m = lax.axis_index("member")
    g = lax.axis_index("grid")
    z, c = g // 2, lax.rem(g, 2)
    other = 1 - c
    points = lat.shape[1]
    width = lat.shape[2]
    sub = points // members
    rows = w_in.shape[0]
    vars_ = w_out.shape[0]
    pad = wo.shape[0]
    latent = w_out.shape[1]
    total = points * planes * 2
    half = width // 2

    mem = (members - 1 - m, m + 1 - 2 * lax.rem(m, 2), m + 2 - 4 * (m // 2), m)
    zed = (z, z + 1 - 2 * lax.rem(z, 2), z + 2 - 4 * (z // 2), planes - 1 - z)

    partner = (m, z * 2 + other)

    def member_dev(s):
        return (mem[s], g)

    def z_dev(k):
        return (m, zed[k] * 2 + c)

    started = []

    def send(src, dst, dev):
        n = len(started)
        copy = pltpu.make_async_remote_copy(
            src_ref=src, dst_ref=dst, send_sem=send_sem.at[n], recv_sem=recv_sem.at[n],
            device_id=dev, device_id_type=pl.DeviceIdType.MESH,
        )
        copy.start()
        started.append(copy)
        return copy

    barrier = pltpu.get_barrier_semaphore()
    peers = [partner] + [z_dev(k) for k in range(1, planes)] + [member_dev(s) for s in (DIAG, ACROSS, DOWN)]
    for dev in peers:
        pl.semaphore_signal(barrier, inc=1, device_id=dev, device_id_type=pl.DeviceIdType.MESH)
    pl.semaphore_wait(barrier, len(peers))

    near = {ACROSS: [], DOWN: []}
    far = []
    to_part = {s: [] for s in range(members)}
    z_copies = [None]

    def block(s, step):
        return w_buf.at[mem[s], zed[step], c]

    def hand_over(s, step):
        to_part[s].append(send(block(s, step), block(s, step), partner))

    def spread_block(step):
        if step > 0:
            z_copies[step].wait_recv()
        if step == 2:
            z_copies.append(send(block(SELF, 2), block(SELF, 2), z_dev(1)))
        src = w_in if step == 0 else block(SELF, step)
        for s in (ACROSS, DOWN):
            near[s].append(send(src, block(SELF, step), member_dev(s)))
        to_part[SELF].append(send(src, block(SELF, step), partner))

    def relay_block(step):
        for s in (ACROSS, DOWN):
            near[s][step].wait_recv()
        s = ACROSS if step % 2 == 0 else DOWN
        far.append(send(block(s, step), block(s, step), member_dev(ACROSS + DOWN - s)))
        hand_over(ACROSS, step)
        hand_over(DOWN, step)

    def far_block(step):
        far[step].wait_recv()
        hand_over(DIAG, step)

    def transpose_next():
        s, copy = loads.pop(0)
        copy.wait()

        def body(t, carry):
            r0 = pl.multiple_of(t * 2 * TILE, 2 * TILE)
            turned = lat[s, pl.ds(r0, 2 * TILE), :].T
            lat_t[0, s, :, pl.ds(r0, 2 * TILE)] = turned[:half]
            lat_t[1, s, :, pl.ds(r0, 2 * TILE)] = turned[half:]
            return carry

        lax.fori_loop(0, points // (2 * TILE), body, 0)

    def contract(slots, first):
        for s in slots:
            for copy in to_part[s]:
                copy.wait_recv()
        big = 4 * TILE

        def body(t, carry):
            r0 = pl.multiple_of(t * big, big)
            acc = b_in[...] if first else gp[pl.ds(r0, big), :]
            for s in slots:
                acc = acc + dot(lat[s, pl.ds(r0, big), :], w_buf[mem[s]].reshape(width, latent), NN)
            gp[pl.ds(r0, big), :] = acc
            return carry

        lax.fori_loop(0, points // big, body, 0)

    z_copies.append(send(w_in, w_buf.at[m, z, c], z_dev(1)))
    z_copies.append(send(w_in, w_buf.at[m, z, c], z_dev(2)))
    spread_block(0)

    own = pltpu.make_async_copy(w_in, w_buf.at[m, z, c], local_sem.at[members])
    own.start()
    loads = []
    for s in (SELF, ACROSS, DOWN, DIAG):
        copy = pltpu.make_async_copy(
            lat_hbm.at[0, :, pl.ds(pl.multiple_of(mem[s] * width, LANES), width)], lat.at[s], local_sem.at[s]
        )
        copy.start()
        loads.append((s, copy))
    tgt_copy = pltpu.make_async_copy(
        tgt_hbm.at[:, pl.ds(pl.multiple_of(m * sub, LANES), sub)], tgt, local_sem.at[members + 1]
    )
    tgt_copy.start()
    small_copies = []
    for n, (src, dst) in enumerate(((b_out_hbm, b_out), (vw_hbm, vw), (w_out_hbm, w_out), (b_in_hbm, b_in))):
        copy = pltpu.make_async_copy(src, dst, local_sem.at[members + 2 + n])
        copy.start()
        small_copies.append(copy)


    wo[...] = jnp.zeros_like(wo)
    for copy in small_copies:
        copy.wait()
    wo[:vars_, :] = w_out[...]
    rowbuf[...] = jnp.zeros_like(rowbuf)
    rowbuf[0:1, :vars_] = b_out[...]
    rowbuf[1:2, :vars_] = vw[...]
    b_col = jnp.broadcast_to(rowbuf[0:1, :], (LANES, LANES)).T[:vars_]
    v_col = jnp.broadcast_to(rowbuf[1:2, :], (LANES, LANES)).T[:vars_]
    lane_sums[...] = jnp.zeros_like(lane_sums)
    ot[...] = jnp.zeros_like(ot)
    sm[...] = jnp.zeros_like(sm)
    csend[...] = jnp.zeros_like(csend)
    own.wait()

    transpose_next()
    relay_block(0)
    spread_block(1)
    transpose_next()
    spread_block(2)
    relay_block(1)
    transpose_next()
    spread_block(3)
    relay_block(2)
    far_block(0)
    transpose_next()
    contract((SELF,), True)
    relay_block(3)
    far_block(1)
    far_block(2)
    contract((ACROSS, DOWN), False)
    far_block(3)
    for copy in to_part[DIAG]:
        copy.wait_recv()

    c0 = math.sqrt(2.0 / math.pi)
    parts = sub // TILE
    f_copies = {}
    eps = DELTA * DELTA
    c_copies = {}
    sums = {"b": jnp.zeros((vars_, LANES), F32), "l": jnp.zeros((vars_, LANES), F32)}

    def activate(part, s):
        r0 = pl.multiple_of(mem[s] * sub + part * TILE, TILE)
        x = dot(lat[DIAG, pl.ds(r0, TILE), :], w_buf[mem[DIAG]].reshape(width, latent), NN)
        x = x + gp[pl.ds(r0, TILE), :]
        sq = x * x
        cdf = 0.5 + 0.5 * jnp.tanh(x * (c0 + (0.044715 * c0) * sq))
        out = x * cdf
        rounded = out.astype(BF)
        act[pl.ds(r0, TILE), :] = rounded
        gp[pl.ds(r0, TILE), :] = cdf + (out * (1.0 - cdf)) * (2.0 * c0 + (6.0 * 0.044715 * c0) * sq)
        return rounded

    def project(part, s, rounded):
        field = dot(wo[...], rounded, NT)
        if s == SELF:
            fown[part] = field[:vars_]
        else:
            peak = jnp.max(jnp.abs(field), axis=0, keepdims=True)
            code = jnp.floor(jnp.sqrt(peak) * 64.0) + 2.0
            scale = (code * code) * (1.0 / 4096.0)
            coded = jnp.round(field * (TOP / scale))
            at = lax.broadcasted_iota(jnp.int32, (pad, TILE), 0)
            coded = jnp.where(at == vars_, jnp.broadcast_to(code, (pad, TILE)), coded)
            fsend[part, s] = coded.astype(jnp.int32).astype(I16)

    def send_field(part, s):
        if s != SELF:
            f_copies[part, s] = send(fsend.at[part, s], frecv.at[part, s], member_dev(s))

    def score(part):
        for s in (DIAG, ACROSS, DOWN):
            f_copies[part, s].wait_recv()
        b_sum, l_sum = sums["b"], sums["l"]
        for at in range(TILE // LANES):
            cols = slice(at * LANES, (at + 1) * LANES)
            first = part * TILE + at * LANES
            place = lax.broadcasted_iota(jnp.int32, (1, LANES), 1) + (g * points + m * sub + first)
            area = jnp.cos(1.4 * (place.astype(F32) + 0.5) / total)
            scale = v_col * area
            f = []
            for s in (DIAG, ACROSS, DOWN):
                coded = frecv[part, s, :, cols].astype(jnp.int32).astype(F32)
                code = coded[vars_:vars_ + 1]
                f.append(coded[:vars_] * ((code * code) * (1.0 / (4096.0 * TOP))))
            f.append(fown[part, :, cols])
            goal = tgt[:, first:first + LANES] - b_col
            pairs = [None] * members
            spread = jnp.zeros((vars_, LANES), F32)
            for i in range(members):
                for j in range(i + 1, members):
                    d = f[i] - f[j]
                    q = d * d + eps
                    inv = lax.rsqrt(q)
                    slope = d * inv
                    spread += q * inv - DELTA
                    pairs[i] = slope if pairs[i] is None else pairs[i] + slope
                    pairs[j] = -slope if pairs[j] is None else pairs[j] - slope
            miss_sum = jnp.zeros((vars_, LANES), F32)
            for s in range(members):
                d = f[s] - goal
                q = d * d + eps
                inv = lax.rsqrt(q)
                miss_sum += q * inv - DELTA
                cot = scale * (d * inv - pairs[s] * (1.0 / (members - 1)))
                b_sum += cot
                if s == SELF:
                    crecv[part, SELF, :vars_, cols] = cot.astype(BF)
                else:
                    csend[part, s, :vars_, cols] = cot.astype(BF)
            l_sum += scale * (miss_sum - spread * (1.0 / (members - 1)))
        sums["b"], sums["l"] = b_sum, l_sum
        for s in (DIAG, ACROSS, DOWN):
            c_copies[part, s] = send(csend.at[part, s], crecv.at[part, s], member_dev(s))

    tgt_copy.wait()
    todo = [(part, s) for part in range(parts) for s in (DIAG, ACROSS, DOWN, SELF)]
    ready = activate(*todo[0])
    for n, (part, s) in enumerate(todo):
        project(part, s, ready)
        if n + 1 < len(todo):
            ready = activate(*todo[n + 1])
        send_field(part, s)
        if s == DOWN and part > 0:
            score(part - 1)
    score(parts - 1)
    lane_sums[:vars_, :] = sums["b"]
    sm[1:2, :LANES] = jnp.sum(lane_sums[...].T, axis=0, keepdims=True)
    sm[1:2, LANES:2 * LANES] = jnp.sum(sums["l"], axis=0, keepdims=True)

    col = jnp.zeros((1, latent), F32)
    for part in range(parts):
        for s in (SELF, ACROSS, DOWN, DIAG):
            if s == ACROSS:
                for k in (ACROSS, DOWN, DIAG):
                    c_copies[part, k].wait_recv()
            r0 = pl.multiple_of(mem[s] * sub + part * TILE, TILE)
            cot_b = crecv[part, s, :vars_]
            d = dot(cot_b, w_out[...], TN) * gp[pl.ds(r0, TILE), :]
            dpre[pl.ds(r0, TILE), :] = d.astype(BF)
            ot[:vars_, :] += dot(cot_b, act[pl.ds(r0, TILE), :], NN)
            col += jnp.sum(d, axis=0, keepdims=True)
    sm[0:1, :] = col

    share = ot.shape[0] // (2 * planes)
    first_half = pl.multiple_of(other * (planes * share), share)
    op_send[...] = ot[pl.ds(first_half, planes * share), :].astype(BF)
    op_copy = send(op_send, op_recv, partner)
    sp_copy = send(sm, sp_recv, partner)

    p_copies = {}
    d_copies = {}
    n_copies = {}
    far_half = 1 - z // 2
    halves = (far_half, z // 2)
    pairs_of = ((DIAG, ACROSS), (DOWN, SELF))

    def chunk(h, pair):
        n = h * 2 + pair
        lo = pair * 2
        left = lat_t[halves[h], lo:lo + 2].reshape(width, points)
        keep[...] = dot(left, dpre[...], NN).reshape(2, 2, 2, rows, latent)
        p_send[n] = keep[:, :, other].astype(BF)
        part_sum[h, lo:lo + 2] = keep[:, :, c]
        p_copies[n] = send(p_send.at[n], p_recv.at[n], partner)

    def fold(h, pair):
        n = h * 2 + pair
        p_copies[n].wait_recv()
        lo = pair * 2
        both = part_sum[h, lo:lo + 2] + p_recv[n].astype(F32)
        if pair == 0:
            d_send[h] = both[0].astype(BF)
            d_copies[h] = [
                send(d_send.at[h, j], d_recv.at[h, j], member_dev(ACROSS + j)) for j in range(2)
            ]
            n_send[h, 0, 0] = both[1, 0].astype(BF)
            part_sum[h, ACROSS, 1] = both[1, 1]
        else:
            n_send[h, 1, 1] = both[0, 1].astype(BF)
            part_sum[h, DOWN, 0] = both[0, 0]
            part_sum[h, SELF] = both[1]

    def direct(h, s):
        j = s - 1
        n_copies[h, s, j] = send(n_send.at[h, j, j], n_recv.at[h, j, j], member_dev(s))

    def relay_sum(h):
        for s, j in ((DOWN, 0), (ACROSS, 1)):
            d_copies[h][j].wait_recv()
            n_send[h, s - 1, j] = (part_sum[h, s, j] + d_recv[h, j].astype(F32)).astype(BF)
            n_copies[h, s, j] = send(n_send.at[h, s - 1, j], n_recv.at[h, s - 1, j], member_dev(s))

    def plane_sum(h):
        for s in (ACROSS, DOWN):
            for j in range(2):
                n_copies[h, s, j].wait_recv()
        part_sum[h, SELF] = (part_sum[h, SELF] + n_recv[h, 0].astype(F32)) + n_recv[h, 1].astype(F32)

    side = lax.rem(z, 2)
    zz_copies = []

    def to_plane(n, value, k):
        z_send[n] = value.astype(BF)
        zz_copies.append(send(z_send.at[n], z_recv.at[n], z_dev(k)))

    def hidden_grad(ch):
        w = w_buf[ch].reshape(width, latent)
        gh[0, :, ch * width:(ch + 1) * width] = dot(dpre[...], w, NT).astype(BF)

    def open_out():
        op_copy.wait_recv()
        mine = pl.multiple_of(c * (planes * share), share)
        om[...] = (ot[pl.ds(mine, planes * share), :] + op_recv[...].astype(F32)).reshape(planes, share, latent)
        om_send[...] = om[...].astype(BF)
        return [send(om_send.at[zed[k]], om_recv.at[k - 1], z_dev(k)) for k in range(1, planes)]

    def cross_out():
        acc = om[z]
        for k in range(1, planes):
            om_copies[k - 1].wait_recv()
            acc += om_recv[k - 1].astype(F32)
        oq[m] = acc.astype(BF)
        return [send(oq.at[m], oq.at[m], member_dev(s)) for s in (DIAG, ACROSS, DOWN)]

    def close_out():
        for copy in oq_copies:
            copy.wait_recv()
        acc = oq[0].astype(F32)
        for k in range(1, members):
            acc += oq[k].astype(F32)
        w2[c, z] = acc.astype(BF)
        return [send(w2.at[c, z], w2.at[c, z], z_dev(k)) for k in range(1, planes)]

    chunk(0, 0)
    om_copies = open_out()
    sp_copy.wait_recv()
    smm[m] = sm[...] + sp_recv[...]
    sm_copies = [send(smm.at[m], smm.at[m], member_dev(s)) for s in (DIAG, ACROSS, DOWN)]
    chunk(0, 1)
    fold(0, 0)
    direct(0, ACROSS)
    chunk(1, 0)
    fold(0, 1)
    direct(0, DOWN)
    chunk(1, 1)
    oq_copies = cross_out()
    relay_sum(0)
    hidden_grad(0)
    fold(1, 0)
    direct(1, ACROSS)
    fold(1, 1)
    direct(1, DOWN)
    for copy in sm_copies:
        copy.wait_recv()
    acc = smm[0]
    for k in range(1, members):
        acc += smm[k]
    smz[z] = acc
    sz_copies = [send(smz.at[z], smz.at[z], z_dev(k)) for k in range(1, planes)]
    w2_copies = close_out()
    hidden_grad(1)
    plane_sum(0)
    to_plane(0, part_sum[0, SELF, 1 - side], 1)
    relay_sum(1)
    hidden_grad(2)
    zz_copies[0].wait_recv()
    to_plane(1, part_sum[0, SELF, side] + z_recv[0].astype(F32), 2)
    plane_sum(1)
    to_plane(2, part_sum[1, SELF, 1 - side], 1)
    for copy in w2_copies:
        copy.wait_recv()
    half_copy = send(w2.at[c], w2.at[c], partner)
    hidden_grad(3)
    acc = part_sum[1, SELF, side]

    kappa = 4.0 / math.sqrt(members * total)
    for copy in sz_copies:
        copy.wait_recv()
    small = smz[0]
    for k in range(1, planes):
        small += smz[k]
    small = small * kappa
    g_b1[...] = small[0:1, :]
    g_b2[...] = small[1:2, :vars_]
    g_loss[...] = jnp.sum(small[1:2, LANES:2 * LANES], axis=1, keepdims=True) * (1.0 / (kappa * members * total * vars_))
    half_copy.wait_recv()
    g_w2[...] = w2[...].reshape(2 * planes * share, latent)[:vars_].astype(F32) * kappa
    for n in (1, 2):
        zz_copies[n].wait_recv()
        acc += z_recv[n].astype(F32)
    g_w1[...] = acc * kappa
    for copy in started:
        copy.wait_send()


def store_kernel(*refs):
    count = len(refs) // 2
    copies = []
    for n in range(count):
        copy = pltpu.make_async_copy(refs[n], refs[count + n], refs[2 * count].at[n])
        copy.start()
        copies.append(copy)
    for copy in copies:
        copy.wait()


def fast(latent, w_in, b_in, w_out, b_out, targets, var_weight, plan):
    members = lax.axis_size("member")
    grid = lax.axis_size("grid")
    planes = grid // 2
    points, width = latent.shape[1], latent.shape[2]
    rows = w_in.shape[0]
    vars_ = w_out.shape[0]
    sub = points // members
    cw = width // members
    parts = sub // TILE
    share = 16 * pl.cdiv(vars_, 32 * planes)
    pad = 8 * pl.cdiv(vars_ + 1, 8)
    n_sems = (planes - 1) * 4 + planes * 10 + (members - 1) * (4 + 2 * parts) + 2 * members + 24
    vmem = pl.BlockSpec(memory_space=pltpu.VMEM)
    hbm = pl.BlockSpec(memory_space=pl.ANY)
    V = pltpu.VMEM
    block = (rows, width)
    scratch = [
        V((members, points, cw), BF), V((2, members, cw // 2, points), BF), V((members, planes, 2, *block), BF),
        V((points, width), F32), V((points, width), BF), V((points, width), BF),
        V((1, width), F32), V((vars_, width), BF), V((1, vars_), F32), V((1, vars_), F32),
        V((pad, width), BF), V((parts, vars_, TILE), F32),
        V((parts, members - 1, pad, TILE), I16), V((parts, members - 1, pad, TILE), I16),
        V((parts, members - 1, pad, TILE), BF), V((parts, members, pad, TILE), BF), V((vars_, sub), F32),
        V((8, LANES), F32), V((LANES, LANES), F32),
        V((2 * planes * share, width), F32), V((planes * share, width), BF), V((planes * share, width), BF),
        V((planes, share, width), F32), V((planes, share, width), BF), V((planes - 1, share, width), BF),
        V((members, share, width), BF), V((2, planes, share, width), BF),
        V((2, width), F32), V((2, width), F32), V((members, 2, width), F32), V((planes, 2, width), F32),
        V((2, 2, 2, *block), F32), V((2, members, 2, *block), F32),
        V((4, 2, 2, *block), BF), V((4, 2, 2, *block), BF),
        V((2, 2, *block), BF), V((2, 2, *block), BF), V((2, 2, 2, *block), BF), V((2, 2, 2, *block), BF),
        V((planes - 1, *block), BF), V((planes - 1, *block), BF),
        pltpu.SemaphoreType.DMA((n_sems,)), pltpu.SemaphoreType.DMA((n_sems,)),
        pltpu.SemaphoreType.DMA((members + 6,)),
    ]
    S = jax.ShapeDtypeStruct
    shapes = [
        ((1, points, width), BF), ((rows, width), F32), ((1, width), F32),
        ((vars_, width), F32), ((1, vars_), F32), ((1, 1), F32),
    ]
    held = pl.pallas_call(
        functools.partial(head_kernel, members, planes),
        out_shape=[pltpu.VMEM(*s) for s in shapes],
        in_specs=[hbm] * 7,
        out_specs=[vmem] * len(shapes),
        scratch_shapes=scratch,
        compiler_params=pltpu.CompilerParams(
            collective_id=0, has_side_effects=True, vmem_limit_bytes=57000 * 1024
        ),
    )(latent, w_in, b_in[None], w_out, b_out[None], targets, var_weight[None])
    gh, g_w1, g_b1, g_w2, g_b2, g_loss = pl.pallas_call(
        store_kernel,
        out_shape=[S(*s) for s in shapes],
        in_specs=[hbm] * len(shapes),
        out_specs=[hbm] * len(shapes),
        scratch_shapes=[pltpu.SemaphoreType.DMA((len(shapes),))],
        compiler_params=pltpu.CompilerParams(has_side_effects=True, vmem_limit_bytes=1024 * 1024),
    )(*[pltpu.with_memory_space_constraint(h, pltpu.VMEM) for h in held])
    return g_loss[0, 0], gh, g_w1, g_b1[0], g_w2, g_b2[0]


def local(latent, w_in, b_in, w_out, b_out, targets, var_weight, plan):
    members = lax.axis_size("member")
    grid = lax.axis_size("grid")
    points, width = latent.shape[1], latent.shape[2]
    whole_plan = plan.shape[0] == members - 1
    tiled = (
        w_in.shape[0] % 16 == 0 and grid == 8 and members == 4
        and points % (members * TILE) == 0 and width % (2 * members * LANES) == 0
        and width // members == grid * w_in.shape[0] and w_out.shape[0] < LANES
        and points * width <= 2048 * 1024
    )
    run = fast if whole_plan and tiled else shards
    return run(latent, w_in, b_in, w_out, b_out, targets, var_weight, plan)


def solution(mesh):
    placed = (
        P("member", "grid", None),
        P(("member", "grid"), None),
        P(),
        P(),
        P(),
        P(None, "grid"),
        P(),
        P(),
    )
    return jax.shard_map(
        local,
        mesh=mesh,
        in_specs=placed,
        out_specs=(P(), P("member", "grid", None), P(("member", "grid"), None), P(), P(), P()),
        check_vma=False,
    )
```
